128 devices in a mesh: event: 8 (over z, core), slab: 16 (over y, x).
Axes of the slice: x: 4, y: 4, z: 4, core: 2. Of those that a mesh axis runs over, the one named last changes fastest.
Arguments:
- wave_prev: float32 [8, 512, 128, 128], P('event', 'slab'), may hold values from -6 to 6
- wave_now: float32 [8, 512, 128, 128], P('event', 'slab'), may hold values from -6 to 6
- adjoint: float32 [8, 4, 512, 128, 128], P('event', None, 'slab'), may hold values from -6 to 6
- background: float32 [8, 512, 128, 128], P('event', 'slab'), may hold values from 0.02 to 0.12
- coeffs_x: float32 [8, 512, 9], P('event', 'slab'), may hold values from -2 to 2
- stiff_y: float32 [128, 128], replicated, may hold values from -0.5 to 0.5
- stiff_z: float32 [128, 128], replicated, may hold values from -0.5 to 0.5
- interp_y: bfloat16 [16, 32], replicated, may hold values from -1.5 to 1.5
- interp_z: bfloat16 [128, 128], replicated, may hold values from -0.5 to 0.5
- model: bfloat16 [2048, 16, 128], P(('event', 'slab')), may hold values from -1.796875 to 1.796875
- block_index: int32 [8, 512, 4], P('event', 'slab'), may hold values from 0 to 2047, as said below
- live_count: int32 [8, 16], P('event', 'slab'), may hold values from 1 to 128, as said below
Outputs:
- wave_last: float32 [8, 512, 128, 128], P('event', 'slab')
- model_gradient: float32 [2048, 16, 128], P(('event', 'slab'))
The draws below stay inside these ranges and needn't reach their ends.
Inputs may be any that keep to these rules, and one draw needn't show every extreme that they name: `block_index`: within one slab of one event, at most 2 tiles name blocks owned by one device, and some device owns exactly 2 of them. `live_count`: some slab has all 128 tiles live.
All inputs are finite; a program needn't handle non-finite values.
Results may differ from the reference program's by a relative error of at most 0.0029.
Values may be sent and summed in bfloat16 or wider, within the bound.
A program may use at most 128 MiB of HBM per device.

```python
import math
import jax
import jax.numpy as jnp
from jax import lax

PL = 32
NY = 128
NZ = 128
REACH = 4
STEPS = 4
QY = 4
BY = 16
BZ = 128
EVENTS = 8
NX = 512
TY = 32
CAP = 2
BLK_DEV = 16
MB = 2048
N_EVENT = 8
N_SLAB = 16
DEVICES = 128


def draw_block_index(key, part):
    n_tiles = PL * QY
    subkeys = jax.random.split(jax.random.fold_in(key, 11), N_EVENT * N_SLAB)

    def one_slab(slab_key):
        first_key, second_key, third_key, fourth_key = jax.random.split(slab_key, 4)
        shuffled = jax.random.permutation(first_key, DEVICES)
        others = jax.random.permutation(second_key, (DEVICES - 1) * CAP)[:n_tiles - CAP]
        chosen = jnp.concatenate([jnp.zeros((CAP,), jnp.int32), (1 + others // CAP).astype(jnp.int32)])
        owners = shuffled[chosen]
        owners = owners[jax.random.permutation(third_key, n_tiles)]
        local_ids = jax.random.randint(fourth_key, (n_tiles,), 0, BLK_DEV)
        return (owners * BLK_DEV + local_ids).astype(jnp.int32)
    block_ids = jax.vmap(one_slab)(subkeys)
    return block_ids.reshape(N_EVENT, N_SLAB * PL, QY)


def draw_live_count(key, part):
    first_key, second_key = jax.random.split(jax.random.fold_in(key, 23))
    counts = jax.random.randint(first_key, (N_EVENT * N_SLAB,), 1, PL * QY + 1)
    full_dev = jax.random.randint(second_key, (), 0, N_EVENT * N_SLAB)
    counts = jnp.where(jnp.arange(N_EVENT * N_SLAB) == full_dev, PL * QY, counts)
    return counts.reshape(N_EVENT, N_SLAB).astype(jnp.int32)


def level_of(rng, extent, shards, least, largest):
    def one(axis_at, parts):
        steps = jax.random.uniform(jax.random.fold_in(jax.random.fold_in(rng, 6), axis_at), (parts,), jnp.float32, least / len(shards), largest / len(shards))
        return jnp.repeat(jnp.exp(steps), extent[axis_at] // parts).reshape((-1,) + (1,) * (len(extent) - axis_at - 1))

    factor_of = one(*shards[0])
    for cut in shards[1:]:
        factor_of = factor_of * one(*cut)
    return factor_of


def noise(key, extent, spread, most, cuts=(), kind=jnp.bfloat16):
    drawn = jax.random.normal(key, extent, jnp.float32) * spread
    if len(cuts) > 0:
        drawn = level_of(key, extent, cuts, -0.22, 0.18) * drawn
    return jnp.clip(drawn, min=-most, max=most).astype(kind)


def setup_inputs(seed: int = 0) -> dict:
    arg_keys = jax.random.split(jax.random.key(seed), 13)
    wave_prev = noise(arg_keys[0], (EVENTS, NX, NY, NZ), 1.0, 6.0, ((0, 8), (1, 16)), jnp.float32)
    wave_now = noise(arg_keys[1], (EVENTS, NX, NY, NZ), 1.0, 6.0, ((0, 8), (1, 16)), jnp.float32)
    adjoint = noise(arg_keys[2], (EVENTS, STEPS, NX, NY, NZ), 1.0, 6.0, ((0, 8), (2, 16)), jnp.float32)
    background = jnp.clip(jnp.exp(math.log(0.12) - 1.7917595 * jax.random.uniform(arg_keys[3], (EVENTS, NX, NY, NZ), jnp.float32) ** level_of(arg_keys[3], (EVENTS, NX, NY, NZ), ((0, 8), (1, 16)), -0.2, 0.2)), 0.02, 0.12)
    coeffs_x = noise(arg_keys[4], (EVENTS, NX, 2 * REACH + 1), (2 * REACH + 1) ** -0.5, 2.0, ((0, 8), (1, 16)), jnp.float32)
    stiff_y = noise(arg_keys[5], (NY, NY), NY ** -0.5, 0.5, (), jnp.float32)
    stiff_z = noise(arg_keys[6], (NZ, NZ), NZ ** -0.5, 0.5, (), jnp.float32)
    interp_y = noise(arg_keys[7], (BY, TY), BY ** -0.5, 1.5)
    interp_z = noise(arg_keys[8], (BZ, NZ), BZ ** -0.5, 0.5)
    model = noise(arg_keys[9], (MB, BY, BZ), 0.3, 1.796875, ((0, 128),))
    block_index = draw_block_index(jax.random.fold_in(arg_keys[12], 71), 0)
    live_count = draw_live_count(jax.random.fold_in(arg_keys[12], 71), 0)
    return dict(wave_prev=wave_prev, wave_now=wave_now, adjoint=adjoint, background=background, coeffs_x=coeffs_x, stiff_y=stiff_y, stiff_z=stiff_z, interp_y=interp_y, interp_z=interp_z, model=model, block_index=block_index, live_count=live_count)


HIGH = lax.Precision.HIGHEST


def stiffness(wavefield, coeffs, stiff_y, stiff_z):
    half_width = (coeffs.shape[-1] - 1) // 2
    n_planes = wavefield.shape[0]
    padded = jnp.pad(wavefield, ((half_width, half_width), (0, 0), (0, 0)))
    result = jnp.einsum("yw,xwz->xyz", stiff_y, wavefield, precision=HIGH)
    result = result + jnp.einsum("xyw,zw->xyz", wavefield, stiff_z, precision=HIGH)
    for offset in range(2 * half_width + 1):
        result = result + coeffs[:, offset][:, None, None] * padded[offset:offset + n_planes]
    return result


def interpolate(blocks, interp_y, interp_z):
    n_tiles = blocks.shape[0]
    along_z = jnp.dot(blocks.reshape(-1, blocks.shape[2]), interp_z, preferred_element_type=jnp.float32)
    along_z = along_z.reshape(n_tiles, blocks.shape[1], -1)
    return jnp.einsum("by,tbz->tyz", interp_y.astype(jnp.float32), along_z, precision=HIGH)


def transpose_interp(kernel_low, interp_y, interp_z, n_tiles):
    rows_tile = interp_y.shape[1]
    back_z = jnp.dot(kernel_low.reshape(-1, kernel_low.shape[2]), interp_z.T, preferred_element_type=jnp.float32)
    back_z = back_z.reshape(n_tiles, rows_tile, -1)
    return jnp.einsum("by,tyc->tbc", interp_y.astype(jnp.float32), back_z, precision=HIGH)


def reference(wave_prev, wave_now, adjoint, background, coeffs_x, stiff_y, stiff_z, interp_y, interp_z, model, block_index, live_count):
    def one_event(inputs):
        prev_w, now_w, adj_w, back_w, coeffs, block_ids, counts = inputs
        n_planes = now_w.shape[0]
        per_slab = n_planes // N_SLAB
        blocks = model[block_ids.reshape(-1)]
        perturb = interpolate(blocks, interp_y, interp_z).reshape(n_planes, NY, NZ)
        tile_num = (jnp.arange(n_planes, dtype=jnp.int32) % per_slab)[:, None] * QY + jnp.arange(QY, dtype=jnp.int32)[None, :]
        slab_of = jnp.arange(n_planes, dtype=jnp.int32) // per_slab
        alive = tile_num < counts[slab_of][:, None]
        alive_rows = jnp.repeat(alive, TY, axis=1)[:, :, None]
        speed_sq = back_w * jnp.exp(jnp.where(alive_rows, perturb, jnp.zeros_like(perturb)))
        kernel = jnp.zeros_like(now_w)
        for time_step in range(STEPS):
            stiff_u = stiffness(now_w, coeffs, stiff_y, stiff_z)
            kernel = kernel - adj_w[time_step] * speed_sq * stiff_u
            prev_w, now_w = now_w, 2.0 * now_w - prev_w - speed_sq * stiff_u
        gradients = transpose_interp(kernel.astype(jnp.bfloat16), interp_y, interp_z, n_planes * QY)
        gradients = gradients * alive.reshape(-1)[:, None, None].astype(gradients.dtype)
        return now_w, gradients

    wave_last, gradients = lax.map(one_event, (wave_prev, wave_now, adjoint, background, coeffs_x, block_index, live_count))
    n_blocks = model.shape[0]
    summed = jax.ops.segment_sum(gradients.reshape(-1, BY * BZ), block_index.reshape(-1), num_segments=n_blocks)
    return wave_last, summed.reshape(n_blocks, BY, BZ)
```

```python
import functools

import jax
import jax.numpy as jnp
from jax import lax
from jax.experimental import pallas as pl
from jax.experimental.pallas import tpu as pltpu
from jax.sharding import PartitionSpec as P

F32 = jnp.float32
BF16 = jnp.bfloat16
I32 = jnp.int32
MESH = pl.DeviceIdType.MESH
ROWS = 8
LANES = 128


def split(value):
    high = value.astype(BF16)
    low = (value - high.astype(F32)).astype(BF16)
    return high, low


def iota(shape, dim):
    return lax.broadcasted_iota(I32, shape, dim)


def dot(a, b):
    return jnp.dot(a, b, preferred_element_type=F32)


def window_kernel(
    cfg,
    prev_hbm,
    now_hbm,
    adj_hbm,
    back_hbm,
    coeffs,
    live,
    stiff_y,
    stiff_z,
    interp_y,
    interp_z,
    model,
    ids_in,
    wave_out,
    grad_out,
    u_a,
    u_b,
    u_hl,
    speed,
    kern,
    adj,
    ku0,
    halo,
    w_y,
    w_z,
    w_fwd,
    w_bwd,
    w_iz,
    id_one,
    id_two,
    id_all,
    idx_own,
    idx_req,
    own_sm,
    req_sm,
    f_a,
    f_b,
    f_ra,
    f_rb,
    f_in,
    tiles,
    g_tiles,
    g_a,
    g_b,
    g_ra,
    g_rb,
    g_in,
    one_hot,
    load_sem,
    idx_sem,
    id1_send,
    id1_recv,
    id2_send,
    id2_recv,
    h_send,
    h_recv,
    fa1_send,
    fa1_recv,
    fa2_send,
    fa2_recv,
    fb1_send,
    fb1_recv,
    fb2_send,
    fb2_recv,
    f_loc,
    ga1_send,
    ga1_recv,
    ga2_send,
    ga2_recv,
    gb1_send,
    gb1_recv,
    gb2_send,
    gb2_recv,
    g_loc,
    out_sem,
):
    ne, ns, planes, reach, steps, n_tiles, rows_t, blk, rows_b = cfg
    nb = ne * ns
    e = lax.axis_index("event")
    s = lax.axis_index("slab")
    own_dev = e * ns + s

    load_now = pltpu.make_async_copy(now_hbm.at[0], u_a.at[pl.ds(reach, planes)], load_sem.at[0])
    load_prev = pltpu.make_async_copy(prev_hbm.at[0], u_b.at[pl.ds(reach, planes)], load_sem.at[1])
    load_back = pltpu.make_async_copy(back_hbm.at[0], speed, load_sem.at[2])
    load_adj = [
        pltpu.make_async_copy(adj_hbm.at[0, i], adj.at[i], load_sem.at[3 + i]) for i in range(steps)
    ]
    load_now.start()
    load_prev.start()
    load_back.start()

    barrier = pltpu.get_barrier_semaphore()
    for d in range(1, ne):
        pl.semaphore_signal(
            barrier, inc=1, device_id=(lax.rem(e + d, ne), s), device_id_type=MESH
        )
    for d in range(1, ns):
        pl.semaphore_signal(
            barrier, inc=1, device_id=(e, lax.rem(s + d, ns)), device_id_type=MESH
        )
    pl.semaphore_wait(barrier, ne - 1 + ns - 1)

    def event_copy(src, dst, send, recv, d):
        return pltpu.make_async_remote_copy(
            src_ref=src,
            dst_ref=dst,
            send_sem=send.at[d],
            recv_sem=recv.at[d],
            device_id=(lax.rem(e + d, ne), s),
            device_id_type=MESH,
        )

    def slab_copy(src, dst, send, recv, d):
        return pltpu.make_async_remote_copy(
            src_ref=src,
            dst_ref=dst,
            send_sem=send.at[d],
            recv_sem=recv.at[d],
            device_id=(e, lax.rem(s + d, ns)),
            device_id_type=MESH,
        )

    ids = jnp.broadcast_to(ids_in[...], (ROWS, LANES))
    id_one[e] = ids
    hop1 = [event_copy(id_one.at[e], id_one.at[e], id1_send, id1_recv, d) for d in range(1, ne)]
    for c in hop1:
        c.start()
    for c in load_adj:
        c.start()

    ids_full = jnp.broadcast_to(ids_in[...], (LANES, LANES))
    owners = lax.shift_right_arithmetic(ids_full, cfg_shift(blk))
    owners_t = jnp.transpose(owners)
    row_i = iota((LANES, LANES), 0)
    lane_i = iota((LANES, LANES), 1)
    earlier = jnp.where((owners == owners_t) & (row_i < lane_i), 1, 0)
    rank = jnp.sum(earlier, axis=0, keepdims=True)
    owner_row = owners[0:1]
    at_e = owner_row // ns
    at_s = owner_row - at_e * ns
    live_n = live[0, 0]
    lane_row = iota((1, LANES), 1)
    address = jnp.where(rank == 0, at_s * ne + at_e, nb + owner_row)
    address = jnp.where(lane_row < live_n, address, 2 * nb)
    none = LANES
    match = owners == row_i
    first = jnp.min(jnp.where(match, lane_i, none), axis=1, keepdims=True)
    second = jnp.min(jnp.where(match & (lane_i > first), lane_i, none), axis=1, keepdims=True)

    def as_row(column):
        return jnp.transpose(jnp.broadcast_to(column, (LANES, LANES)))[0:1]

    tile_0 = as_row(first)
    tile_1 = as_row(second)
    tile_0 = jnp.where(tile_0 < live_n, tile_0, n_tiles)
    tile_1 = jnp.where(tile_1 < live_n, tile_1, n_tiles)
    sub = iota((ROWS, LANES), 0)
    table = jnp.where(
        sub == 0,
        jnp.broadcast_to(address, (ROWS, LANES)),
        jnp.where(
            sub == 1,
            jnp.broadcast_to(tile_0, (ROWS, LANES)),
            jnp.broadcast_to(tile_1, (ROWS, LANES)),
        ),
    )
    idx_own[...] = table
    own_copy = pltpu.make_async_copy(idx_own, own_sm, idx_sem.at[0])
    own_copy.start()

    high, low = split(stiff_y[...])
    w_y[...] = jnp.concatenate(
        [jnp.concatenate([high, high], axis=1), jnp.concatenate([low, low], axis=1)], axis=0
    )
    high, low = split(jnp.transpose(stiff_z[...]))
    half = jnp.concatenate([high, low], axis=1)
    w_z[...] = jnp.concatenate([half, half], axis=0)

    for c in hop1:
        c.wait()
    gathered = jnp.full((ROWS, LANES), -1, I32)
    for i in range(ne):
        gathered = jnp.where(sub == i, id_one[i], gathered)
    id_two[...] = gathered
    for i in range(LANES // ROWS):
        if i >= ns:
            id_all[i] = jnp.full((ROWS, LANES), -1, I32)
    id_all[s] = gathered
    hop2 = [slab_copy(id_two, id_all.at[s], id2_send, id2_recv, d) for d in range(1, ns)]
    for c in hop2:
        c.start()

    load_now.wait()
    zero_halo = jnp.zeros((reach,) + u_a.shape[1:], F32)
    for buf in (u_a, u_b):
        buf[pl.ds(0, reach)] = zero_halo
        buf[pl.ds(reach + planes, reach)] = zero_halo

    def split_planes(i, carry):
        high, low = split(u_a[reach + i])
        u_hl[i, 0] = high
        u_hl[i, 1] = low
        return carry

    lax.fori_loop(0, planes, split_planes, 0)

    def halo_copy(step, side):
        start = 0 if side == 0 else planes - reach
        return pltpu.make_async_remote_copy(
            src_ref=u_hl.at[pl.ds(start, reach), 0],
            dst_ref=halo.at[step, side],
            send_sem=h_send.at[step, side],
            recv_sem=h_recv.at[step, side],
            device_id=(e, lax.rem(s + (ns - 1 if side == 0 else 1), ns)),
            device_id_type=MESH,
        )

    def send_halos(step):
        @pl.when(s > 0)
        def _():
            halo_copy(step, 0).start()

        @pl.when(s < ns - 1)
        def _():
            halo_copy(step, 1).start()

    def take_halos(step, buf):
        @pl.when(s > 0)
        def _():
            halo_copy(step, 0).wait_send()
            halo_copy(step, 1).wait_recv()
            buf[pl.ds(0, reach)] = halo[step, 1].astype(F32)

        @pl.when(s < ns - 1)
        def _():
            halo_copy(step, 1).wait_send()
            halo_copy(step, 0).wait_recv()
            buf[pl.ds(reach + planes, reach)] = halo[step, 0].astype(F32)

    send_halos(0)

    for c in hop2:
        c.wait()
    asked_all = id_all[...].reshape(LANES, LANES)
    mine = lax.shift_right_arithmetic(asked_all, cfg_shift(blk)) == own_dev
    code = lane_i * blk + (asked_all & (blk - 1))
    none = LANES * blk
    code_0 = jnp.min(jnp.where(mine, code, none), axis=1, keepdims=True)
    code_1 = jnp.min(jnp.where(mine & (code > code_0), code, none), axis=1, keepdims=True)
    asked_0 = as_row(code_0) & (blk - 1)
    asked_1 = as_row(code_1) & (blk - 1)
    idx_req[...] = jnp.where(
        sub == 0,
        jnp.broadcast_to(asked_0, (ROWS, LANES)),
        jnp.broadcast_to(asked_1, (ROWS, LANES)),
    )
    req_copy = pltpu.make_async_copy(idx_req, req_sm, idx_sem.at[1])
    req_copy.start()
    req_copy.wait()

    def find_blocks(i, carry):
        for j in range(ne):
            f_a[j, i] = model[req_sm[0, i * ROWS + j]]
            f_b[i, j] = model[req_sm[1, i * ROWS + j]]
        return carry

    lax.fori_loop(0, ns, find_blocks, 0)

    def exchange(a, b, ra, rb, out, sems, loc):
        a1s, a1r, a2s, a2r, b1s, b1r, b2s, b2r = sems
        a1 = [
            event_copy(a.at[lax.rem(e + d, ne)], ra.at[e], a1s, a1r, d) for d in range(1, ne)
        ]
        b1 = [slab_copy(b.at[lax.rem(s + d, ns)], rb.at[s], b1s, b1r, d) for d in range(1, ns)]
        here = [
            pltpu.make_async_copy(a.at[e], ra.at[e], loc.at[0]),
            pltpu.make_async_copy(b.at[s], rb.at[s], loc.at[1]),
        ]
        a2 = [
            slab_copy(
                ra.at[:, lax.rem(s + d, ns)], out.at[pl.ds(s * ne, ne)], a2s, a2r, d
            )
            for d in range(1, ns)
        ]
        b2 = [
            event_copy(
                rb.at[:, lax.rem(e + d, ne)], out.at[pl.ds(nb + e * ns, ns)], b2s, b2r, d
            )
            for d in range(1, ne)
        ]
        there = [
            pltpu.make_async_copy(ra.at[:, s], out.at[pl.ds(s * ne, ne)], loc.at[2]),
            pltpu.make_async_copy(rb.at[:, e], out.at[pl.ds(nb + e * ns, ns)], loc.at[3]),
        ]

        def begin():
            for c in a1 + b1 + here:
                c.start()

        def middle():
            for c in here[:1] + a1:
                c.wait()
            for c in a2 + there[:1]:
                c.start()
            for c in here[1:] + b1:
                c.wait()
            for c in b2 + there[1:]:
                c.start()

        def end():
            for c in a2 + b2 + there:
                c.wait()

        return begin, middle, end

    begin, middle, end = exchange(
        f_a,
        f_b,
        f_ra,
        f_rb,
        f_in,
        (fa1_send, fa1_recv, fa2_send, fa2_recv, fb1_send, fb1_recv, fb2_send, fb2_recv),
        f_loc,
    )
    begin()

    tiles_y = LANES // rows_t
    half_rows = tiles_y * rows_b
    pick_b = jnp.where(iota((half_rows, rows_b), 0) % rows_b == iota((half_rows, rows_b), 1), 1.0, 0.0)
    pick_y = jnp.where(iota((rows_t, LANES), 1) % rows_t == iota((rows_t, LANES), 0), 1.0, 0.0)
    wide = dot(pick_b.astype(BF16), interp_y[...]).astype(BF16)
    wide = dot(wide, pick_y.astype(BF16))
    on_diag = iota((half_rows, LANES), 0) // rows_b == iota((half_rows, LANES), 1) // rows_t
    diag = jnp.where(on_diag, wide, 0.0)
    w_bwd[...] = diag.astype(BF16)
    w_fwd[...] = jnp.transpose(jnp.concatenate([diag, diag], axis=0)).astype(BF16)
    iz_t = jnp.transpose(interp_z[...].astype(F32)).astype(BF16)
    w_iz[...] = jnp.concatenate([iz_t, iz_t], axis=0)

    ny = LANES

    def stiff_pair(x):
        a, b = u_hl[x, 0], u_hl[x, 1]
        c, d = u_hl[x + 1, 0], u_hl[x + 1, 1]
        left = jnp.concatenate(
            [jnp.concatenate([a, b], axis=1), jnp.concatenate([c, d], axis=1)], axis=0
        )
        right = jnp.concatenate(
            [jnp.concatenate([a, c], axis=1), jnp.concatenate([b, d], axis=1)], axis=0
        )
        along_z = dot(left, w_z[...])
        along_z = along_z[:, :LANES] + along_z[:, LANES:]
        along_y = dot(w_y[...], right)
        along_y = along_y[:ny] + along_y[ny:]
        return along_z[:ny] + along_y[:, :LANES], along_z[ny:] + along_y[:, LANES:]

    def stencil(buf, x):
        total = coeffs[0, x, 0] * buf[x]
        for k in range(1, 2 * reach + 1):
            total = total + coeffs[0, x, k] * buf[x + k]
        return total

    pairs = planes // 2
    edge = reach // 2

    def over_planes(body, before_edges):
        def interior(i, carry):
            body(2 * i)
            return carry

        lax.fori_loop(edge, pairs - edge, interior, 0)
        before_edges()

        def edges(i, carry):
            body(2 * jnp.where(i < edge, i, pairs - 2 * edge + i))
            return carry

        lax.fori_loop(0, 2 * edge, edges, 0)

    def first_stiff(x):
        for p, part in enumerate(stiff_pair(x)):
            ku0[x + p] = part + stencil(u_a, x + p)

    over_planes(first_stiff, lambda: take_halos(0, u_a))
    middle()
    f_in[2 * nb] = jnp.zeros(f_in.shape[1:], BF16)

    ids_f = jnp.where(
        sub == 0,
        jnp.broadcast_to(asked_0, (ROWS, LANES)),
        jnp.broadcast_to(asked_1, (ROWS, LANES)),
    ).astype(F32).astype(BF16)

    slots = ns * ne

    def spread(rank_row, position, base):
        width = slots * rows_b
        chunk = min(512, width)
        for c0 in range(0, width, chunk):
            lane = iota((LANES, chunk), 1) + c0
            source = position(lane // rows_b)
            pick = jnp.where(iota((LANES, chunk), 0) == source, 1.0, 0.0).astype(BF16)
            key = dot(ids_f, pick)[rank_row : rank_row + 1].astype(I32) * rows_b
            key = key + (iota((1, chunk), 1) + c0) % rows_b
            rows = blk * rows_b
            hot = jnp.where(
                jnp.broadcast_to(key, (rows, chunk)) == iota((rows, chunk), 0), 1.0, 0.0
            )
            one_hot[:, base + c0 : base + c0 + chunk] = hot.astype(BF16)

    spread(0, lambda slot: (slot // ne) * ROWS + slot % ne, 0)
    spread(1, lambda slot: (slot % ns) * ROWS + slot // ns, slots * rows_b)

    own_copy.wait()
    load_back.wait()
    load_prev.wait()
    end()

    def take_tile(i, carry):
        tiles[i] = f_in[own_sm[0, i]]
        return carry

    lax.fori_loop(0, n_tiles, take_tile, 0, unroll=8)

    def speed_pair(i, carry):
        x = 2 * i
        blocks = tiles[pl.ds(x * tiles_y, 2 * tiles_y)].reshape(2 * half_rows, LANES)
        high, low = split(dot(blocks, interp_z[...]))
        right = jnp.concatenate(
            [
                jnp.concatenate([high[:half_rows], high[half_rows:]], axis=1),
                jnp.concatenate([low[:half_rows], low[half_rows:]], axis=1),
            ],
            axis=0,
        )
        perturb = dot(w_fwd[...], right)
        speed[x] = speed[x] * jnp.exp(perturb[:, :LANES])
        speed[x + 1] = speed[x + 1] * jnp.exp(perturb[:, LANES:])
        return carry

    lax.fori_loop(0, pairs, speed_pair, 0)

    def advance(x, force, step, now, prev):
        change = speed[x] * force
        drawn = adj[step, x] * change
        if step == 0:
            kern[x] = -drawn
        elif step < steps - 1:
            kern[x] = kern[x] - drawn
        else:
            total = (kern[x] - drawn).astype(BF16)
            u_hl[x, 1] = total
        later = 2.0 * now[x + reach] - prev[x + reach] - change
        prev[x + reach] = later
        if step < steps - 1:
            high, low = split(later)
            u_hl[x, 0] = high
            u_hl[x, 1] = low

    load_adj[0].wait()

    def first_step(i, carry):
        advance(i, ku0[i], 0, u_a, u_b)
        return carry

    lax.fori_loop(0, planes, first_step, 0)
    if steps > 1:
        send_halos(1)
    now, prev = u_b, u_a
    for step in range(1, steps):
        load_adj[step].wait()

        def body(x):
            parts = stiff_pair(x)
            for p in range(2):
                advance(x + p, parts[p] + stencil(now, x + p), step, now, prev)

        over_planes(body, functools.partial(take_halos, step, now))
        if step < steps - 1:
            send_halos(step + 1)
        now, prev = prev, now

    wave_copy = pltpu.make_async_copy(now.at[pl.ds(reach, planes)], wave_out.at[0], out_sem)
    wave_copy.start()

    def grad_pair(i, carry):
        x = 2 * i
        right = jnp.concatenate([u_hl[x, 1], u_hl[x + 1, 1]], axis=1)
        back = dot(w_bwd[...], right)
        parts = []
        for p in range(2):
            high, low = split(back[:, p * LANES : (p + 1) * LANES])
            parts.append(jnp.concatenate([high, low], axis=1))
        grads = dot(jnp.concatenate(parts, axis=0), w_iz[...])
        g_tiles[pl.ds(x * tiles_y, 2 * tiles_y)] = grads.astype(BF16).reshape(
            2 * tiles_y, rows_b, LANES
        )
        return carry

    lax.fori_loop(0, pairs, grad_pair, 0)
    g_tiles[n_tiles] = jnp.zeros(g_tiles.shape[1:], BF16)

    def pack(i, carry):
        for j in range(ne):
            g_a[j, i] = g_tiles[own_sm[1, j * ns + i]]
            g_b[i, j] = g_tiles[own_sm[2, j * ns + i]]
        return carry

    lax.fori_loop(0, ns, pack, 0)
    begin, middle, end = exchange(
        g_a,
        g_b,
        g_ra,
        g_rb,
        g_in,
        (ga1_send, ga1_recv, ga2_send, ga2_recv, gb1_send, gb1_recv, gb2_send, gb2_recv),
        g_loc,
    )
    begin()
    middle()
    end()
    received = g_in[...].reshape(2 * nb * rows_b, LANES)
    total = dot(one_hot[...], received)
    grad_out[...] = total.reshape(grad_out.shape)
    wave_copy.wait()


def cfg_shift(blk):
    return blk.bit_length() - 1


def shards(
    wave_prev,
    wave_now,
    adjoint,
    background,
    coeffs_x,
    stiff_y,
    stiff_z,
    interp_y,
    interp_z,
    model,
    block_index,
    live_count,
):
    ne = lax.axis_size("event")
    ns = lax.axis_size("slab")
    nb = ne * ns
    blk, rows_b, _ = model.shape
    planes, ny, nz = wave_now.shape[1:]
    steps = adjoint.shape[1]
    reach = (coeffs_x.shape[2] - 1) // 2
    tiles_y = block_index.shape[2]
    n_tiles = planes * tiles_y
    rows_t = ny // tiles_y
    ids = block_index.reshape(1, n_tiles)
    if n_tiles < LANES:
        ids = jnp.pad(ids, ((0, 0), (0, LANES - n_tiles)), constant_values=-1)
    cfg = (ne, ns, planes, reach, steps, n_tiles, rows_t, blk, rows_b)
    dma = pltpu.SemaphoreType.DMA
    vmem = pltpu.VMEM
    slot = (rows_b, nz)

    def buffers():
        return [
            vmem((ne, ns) + slot, BF16),
            vmem((ns, ne) + slot, BF16),
            vmem((ne, ns) + slot, BF16),
            vmem((ns, ne) + slot, BF16),
        ]

    def sems():
        return [dma((n,)) for n in (ne, ne, ns, ns, ns, ns, ne, ne)] + [dma((4,))]

    fetch = buffers()
    grads = buffers()
    whole = pl.BlockSpec(memory_space=pltpu.VMEM)
    smem = pl.BlockSpec(memory_space=pltpu.SMEM)
    hbm = pl.BlockSpec(memory_space=pl.ANY)
    wave, grad = pl.pallas_call(
        functools.partial(window_kernel, cfg),
        out_shape=(
            jax.ShapeDtypeStruct(wave_now.shape, F32),
            jax.ShapeDtypeStruct(model.shape, F32),
        ),
        in_specs=[hbm] * 4 + [smem] * 2 + [whole] * 6,
        out_specs=(hbm, whole),
        scratch_shapes=[
            vmem((planes + 2 * reach, ny, nz), F32),
            vmem((planes + 2 * reach, ny, nz), F32),
            vmem((planes, 2, ny, nz), BF16),
            vmem((planes, ny, nz), F32),
            vmem((planes, ny, nz), F32),
            vmem((steps, planes, ny, nz), F32),
            vmem((planes, ny, nz), F32),
            vmem((steps, 2, reach, ny, nz), BF16),
            vmem((2 * ny, 2 * ny), BF16),
            vmem((2 * nz, 2 * nz), BF16),
            vmem((ny, 2 * tiles_y * rows_b), BF16),
            vmem((tiles_y * rows_b, ny), BF16),
            vmem((2 * nz, nz), BF16),
            vmem((ne, ROWS, LANES), I32),
            vmem((ROWS, LANES), I32),
            vmem((LANES // ROWS, ROWS, LANES), I32),
            vmem((ROWS, LANES), I32),
            vmem((ROWS, LANES), I32),
            pltpu.SMEM((ROWS, LANES), I32),
            pltpu.SMEM((ROWS, LANES), I32),
            *fetch,
            vmem((2 * nb + 1,) + slot, BF16),
            vmem((n_tiles,) + slot, BF16),
            vmem((n_tiles + 1,) + slot, BF16),
            *grads,
            vmem((2 * nb,) + slot, BF16),
            vmem((blk * rows_b, 2 * nb * rows_b), BF16),
            dma((3 + steps,)),
            dma((2,)),
            dma((ne,)),
            dma((ne,)),
            dma((ns,)),
            dma((ns,)),
            dma((steps, 2)),
            dma((steps, 2)),
            *sems(),
            *sems(),
            dma,
        ],
        compiler_params=pltpu.CompilerParams(
            collective_id=0, has_side_effects=True, vmem_limit_bytes=56 * 1024 * 1024
        ),
        name="window",
    )(
        wave_prev,
        wave_now,
        adjoint,
        background,
        coeffs_x,
        live_count,
        stiff_y,
        stiff_z,
        interp_y,
        interp_z,
        model,
        ids,
    )
    return wave, grad


def solution(mesh):
    return jax.shard_map(
        shards,
        mesh=mesh,
        in_specs=(
            P("event", "slab", None, None),
            P("event", "slab", None, None),
            P("event", None, "slab", None, None),
            P("event", "slab", None, None),
            P("event", "slab", None),
            P(),
            P(),
            P(),
            P(),
            P(("event", "slab"), None, None),
            P("event", "slab", None),
            P("event", "slab"),
        ),
        out_specs=(P("event", "slab", None, None), P(("event", "slab"), None, None)),
        check_vma=False,
    )
```

```python
import functools

import jax
import jax.numpy as jnp
from jax import lax
from jax.experimental import pallas as pl
from jax.experimental.pallas import tpu as pltpu
from jax.sharding import PartitionSpec as P

F32 = jnp.float32
BF16 = jnp.bfloat16
I32 = jnp.int32
MESH = pl.DeviceIdType.MESH
ROWS = 8
LANES = 128


def split(value):
    high = value.astype(BF16)
    low = (value - high.astype(F32)).astype(BF16)
    return high, low


def iota(shape, dim):
    return lax.broadcasted_iota(I32, shape, dim)


def dot(a, b):
    return jnp.dot(a, b, preferred_element_type=F32)


def window_kernel(
    cfg,
    prev_hbm,
    now_hbm,
    adj_hbm,
    back_hbm,
    coeffs_hbm,
    live,
    stiff_y,
    stiff_z,
    interp_y,
    interp_z,
    model,
    ids_in,
    wave_out,
    grad_out,
    u_a,
    u_b,
    u_hl,
    speed,
    kern,
    adj,
    ku0,
    halo,
    w_y,
    w_z,
    w_fwd,
    w_bwd,
    w_iz,
    coeffs,
    id_own,
    id_all,
    idx_own,
    idx_req,
    asked_all,
    own_sm,
    req_sm,
    column,
    f_out,
    f_in,
    tiles,
    g_tiles,
    g_a,
    g_b,
    g_ra,
    g_rb,
    g_in,
    one_hot,
    load_sem,
    idx_sem,
    id_send,
    id_recv,
    col_send,
    col_recv,
    ask_send,
    ask_recv,
    f_send,
    f_recv,
    h_send,
    h_recv,
    f_loc,
    ga1_send,
    ga1_recv,
    ga2_send,
    ga2_recv,
    gb1_send,
    gb1_recv,
    gb2_send,
    gb2_recv,
    g_loc,
    out_sem,
):
    ne, ns, planes, reach, steps, n_tiles, rows_t, blk, rows_b = cfg
    nb = ne * ns
    e = lax.axis_index("event")
    s = lax.axis_index("slab")
    tiles_y = LANES // rows_t

    load_now = pltpu.make_async_copy(now_hbm.at[0], u_a.at[pl.ds(reach, planes)], load_sem.at[0])
    load_prev = pltpu.make_async_copy(prev_hbm.at[0], u_b.at[pl.ds(reach, planes)], load_sem.at[1])
    load_back = pltpu.make_async_copy(back_hbm.at[0], speed, load_sem.at[2])
    load_adj = [
        pltpu.make_async_copy(adj_hbm.at[0, i], adj.at[i], load_sem.at[3 + i]) for i in range(steps)
    ]
    load_coeffs = pltpu.make_async_copy(coeffs_hbm, coeffs, idx_sem.at[2])
    load_now.start()
    load_coeffs.start()
    load_prev.start()
    load_back.start()

    barrier = pltpu.get_barrier_semaphore()
    for d in range(1, ne):
        pl.semaphore_signal(
            barrier, inc=1, device_id=(lax.rem(e + d, ne), s), device_id_type=MESH
        )
    for d in range(1, ns):
        pl.semaphore_signal(
            barrier, inc=1, device_id=(e, lax.rem(s + d, ns)), device_id_type=MESH
        )
    pl.semaphore_wait(barrier, ne - 1 + ns - 1)

    def event_copy(src, dst, send, recv, d):
        return pltpu.make_async_remote_copy(
            src_ref=src,
            dst_ref=dst,
            send_sem=send.at[d],
            recv_sem=recv.at[d],
            device_id=(lax.rem(e + d, ne), s),
            device_id_type=MESH,
        )

    def slab_copy(src, dst, send, recv, d):
        return pltpu.make_async_remote_copy(
            src_ref=src,
            dst_ref=dst,
            send_sem=send.at[d],
            recv_sem=recv.at[d],
            device_id=(e, lax.rem(s + d, ns)),
            device_id_type=MESH,
        )

    column_copies = [event_copy(model, column.at[e], col_send, col_recv, d) for d in range(1, ne)]
    sub = iota((ROWS, LANES), 0)
    planes_id = ids_in[0]
    ids_row = jnp.concatenate([planes_id[q : q + 1] for q in range(tiles_y)], axis=1)
    if n_tiles < LANES:
        ids_row = jnp.concatenate([ids_row, jnp.full((1, LANES - n_tiles), -1, I32)], axis=1)
    ids = jnp.broadcast_to(ids_row, (ROWS, LANES))
    id_own[...] = ids
    for i in range(LANES // ROWS):
        if i >= ns:
            id_all[i] = jnp.full((ROWS, LANES), -1, I32)
    id_all[s] = ids
    id_copies = [slab_copy(id_own, id_all.at[s], id_send, id_recv, d) for d in range(1, ns)]
    for c in id_copies:
        c.start()
    for c in column_copies:
        c.start()
    column[e] = model[...]
    for c in load_adj:
        c.start()

    owners = lax.shift_right_arithmetic(jnp.broadcast_to(ids_row, (LANES, LANES)), cfg_shift(blk))
    owners_t = jnp.transpose(owners)
    row_i = iota((LANES, LANES), 0)
    lane_i = iota((LANES, LANES), 1)
    earlier = jnp.where((owners == owners_t) & (row_i < lane_i), 1, 0)
    rank = jnp.sum(earlier, axis=0, keepdims=True)
    owner_row = owners[0:1]
    at_e = owner_row // ns
    at_s = owner_row - at_e * ns
    live_n = live[0, 0]

    def in_order(lane):
        return lane % planes * tiles_y + lane // planes

    address = at_s * (2 * ne) + rank * ne + at_e
    alive = in_order(iota((1, LANES), 1)) < live_n
    address = jnp.where(alive, address, 2 * nb)
    none = LANES
    match = owners == row_i
    first = jnp.min(jnp.where(match, lane_i, none), axis=1, keepdims=True)
    second = jnp.min(jnp.where(match & (lane_i > first), lane_i, none), axis=1, keepdims=True)

    def as_row(values):
        return jnp.transpose(jnp.broadcast_to(values, (LANES, LANES)))[0:1]

    def tile_at(lane):
        tile = in_order(lane)
        return jnp.where((lane < none) & (tile < live_n), tile, n_tiles)

    tile_0 = tile_at(as_row(first))
    tile_1 = tile_at(as_row(second))
    idx_own[...] = jnp.where(
        sub == 0,
        jnp.broadcast_to(address, (ROWS, LANES)),
        jnp.where(
            sub == 1,
            jnp.broadcast_to(tile_0, (ROWS, LANES)),
            jnp.broadcast_to(tile_1, (ROWS, LANES)),
        ),
    )
    own_copy = pltpu.make_async_copy(idx_own, own_sm, idx_sem.at[0])
    own_copy.start()

    high, low = split(stiff_y[...])
    w_y[...] = jnp.concatenate(
        [jnp.concatenate([high, high], axis=1), jnp.concatenate([low, low], axis=1)], axis=0
    )
    high, low = split(jnp.transpose(stiff_z[...]))
    half = jnp.concatenate([high, low], axis=1)
    w_z[...] = jnp.concatenate([half, half], axis=0)

    load_now.wait()

    def split_planes(i, carry):
        high, low = split(u_a[reach + i])
        u_hl[i, 0] = high
        u_hl[i, 1] = low
        return carry

    def halo_copy(step, side):
        start = 0 if side == 0 else planes - reach
        return pltpu.make_async_remote_copy(
            src_ref=u_hl.at[pl.ds(start, reach), 0],
            dst_ref=halo.at[step, side],
            send_sem=h_send.at[step, side],
            recv_sem=h_recv.at[step, side],
            device_id=(e, lax.rem(s + (ns - 1 if side == 0 else 1), ns)),
            device_id_type=MESH,
        )

    def send_halo(step, side):
        @pl.when(s > 0 if side == 0 else s < ns - 1)
        def _():
            halo_copy(step, side).start()

    def take_halo(step, side, buf):
        @pl.when(s > 0 if side == 0 else s < ns - 1)
        def _():
            halo_copy(step, side).wait_send()
            halo_copy(step, 1 - side).wait_recv()
            at = 0 if side == 0 else reach + planes
            buf[pl.ds(at, reach)] = halo[step, 1 - side].astype(F32)

    lax.fori_loop(0, reach, split_planes, 0, unroll=2)
    lax.fori_loop(planes - reach, planes, split_planes, 0, unroll=2)
    send_halo(0, 0)
    send_halo(0, 1)
    lax.fori_loop(reach, planes - reach, split_planes, 0, unroll=2)
    zero_halo = jnp.zeros((reach,) + u_a.shape[1:], F32)
    for buf in (u_a, u_b):
        buf[pl.ds(0, reach)] = zero_halo
        buf[pl.ds(reach + planes, reach)] = zero_halo

    for c in id_copies:
        c.wait()
    asked_ids = id_all[...].reshape(LANES, LANES)
    wanted = (row_i % ROWS) * ns + s
    mine = (lax.shift_right_arithmetic(asked_ids, cfg_shift(blk)) == wanted) & (row_i % ROWS < ne)
    code = lane_i * blk + (asked_ids & (blk - 1))
    none = LANES * blk
    code_0 = jnp.min(jnp.where(mine, code, none), axis=1, keepdims=True)
    code_1 = jnp.min(jnp.where(mine & (code > code_0), code, none), axis=1, keepdims=True)
    asked_0 = as_row(code_0) & (blk - 1)
    asked_1 = as_row(code_1) & (blk - 1)
    asked = jnp.where(
        sub == 0,
        jnp.broadcast_to(asked_0, (ROWS, LANES)),
        jnp.broadcast_to(asked_1, (ROWS, LANES)),
    )
    idx_req[...] = asked
    req_copy = pltpu.make_async_copy(idx_req, req_sm, idx_sem.at[1])
    req_copy.start()
    asked_all[e] = asked
    for c in column_copies:
        c.wait()
    req_copy.wait()
    fetches = []
    for d in [*range(1, ns), 0]:
        to = lax.rem(s + d, ns)
        for j in range(ne):
            f_out[to, j] = column[j, req_sm[0, to * ROWS + j]]
            f_out[to, ne + j] = column[j, req_sm[1, to * ROWS + j]]
        dst = f_in.at[pl.ds(s * (2 * ne), 2 * ne)]
        if d == 0:
            c = pltpu.make_async_copy(f_out.at[to], dst, f_loc)
        else:
            c = slab_copy(f_out.at[to], dst, f_send, f_recv, d)
        c.start()
        fetches.append(c)
    ask_copies = [
        event_copy(idx_req, asked_all.at[e], ask_send, ask_recv, d) for d in range(1, ne)
    ]
    for c in ask_copies:
        c.start()

    def exchange(a, b, ra, rb, out, sems, loc):
        a1s, a1r, a2s, a2r, b1s, b1r, b2s, b2r = sems
        a1 = [
            event_copy(a.at[lax.rem(e + d, ne)], ra.at[e], a1s, a1r, d) for d in range(1, ne)
        ]
        b1 = [slab_copy(b.at[lax.rem(s + d, ns)], rb.at[s], b1s, b1r, d) for d in range(1, ns)]
        here = [
            pltpu.make_async_copy(a.at[e], ra.at[e], loc.at[0]),
            pltpu.make_async_copy(b.at[s], rb.at[s], loc.at[1]),
        ]
        a2 = [
            slab_copy(ra.at[:, lax.rem(s + d, ns)], out.at[0, :, s], a2s, a2r, d)
            for d in range(1, ns)
        ]
        b2 = [
            event_copy(rb.at[:, lax.rem(e + d, ne)], out.at[1, e], b2s, b2r, d)
            for d in range(1, ne)
        ]
        there = [
            pltpu.make_async_copy(ra.at[:, s], out.at[0, :, s], loc.at[2]),
            pltpu.make_async_copy(rb.at[:, e], out.at[1, e], loc.at[3]),
        ]

        def begin():
            for c in a1 + b1 + here:
                c.start()

        def middle():
            for c in here[:1] + a1:
                c.wait()
            for c in a2 + there[:1]:
                c.start()
            for c in here[1:] + b1:
                c.wait()
            for c in b2 + there[1:]:
                c.start()

        def end():
            for c in a2 + b2 + there:
                c.wait()

        return begin, middle, end

    half_rows = tiles_y * rows_b
    pick_b = jnp.where(iota((half_rows, rows_b), 0) % rows_b == iota((half_rows, rows_b), 1), 1.0, 0.0)
    pick_y = jnp.where(iota((rows_t, LANES), 1) % rows_t == iota((rows_t, LANES), 0), 1.0, 0.0)
    wide = dot(pick_b.astype(BF16), interp_y[...]).astype(BF16)
    wide = dot(wide, pick_y.astype(BF16))
    on_diag = iota((half_rows, LANES), 0) // rows_b == iota((half_rows, LANES), 1) // rows_t
    diag = jnp.where(on_diag, wide, 0.0)
    w_bwd[...] = diag.astype(BF16)
    w_fwd[...] = jnp.transpose(jnp.concatenate([diag, diag], axis=0)).astype(BF16)
    iz_t = jnp.transpose(interp_z[...].astype(F32)).astype(BF16)
    w_iz[...] = jnp.concatenate([iz_t, iz_t], axis=0)

    ny = LANES

    def stiff_pair(x):
        a, b = u_hl[x, 0], u_hl[x, 1]
        c, d = u_hl[x + 1, 0], u_hl[x + 1, 1]
        left = jnp.concatenate(
            [jnp.concatenate([a, b], axis=1), jnp.concatenate([c, d], axis=1)], axis=0
        )
        right = jnp.concatenate(
            [jnp.concatenate([a, c], axis=1), jnp.concatenate([b, d], axis=1)], axis=0
        )
        along_z = dot(left, w_z[...])
        along_z = along_z[:, :LANES] + along_z[:, LANES:]
        along_y = dot(w_y[...], right)
        along_y = along_y[:ny] + along_y[ny:]
        return along_z[:ny] + along_y[:, :LANES], along_z[ny:] + along_y[:, LANES:]

    def stencil(buf, x):
        total = coeffs[0, 0, x] * buf[x]
        for k in range(1, 2 * reach + 1):
            total = total + coeffs[k, 0, x] * buf[x + k]
        return total

    pairs = planes // 2
    edge = reach // 2

    def over_interior(body):
        def interior(i, carry):
            body(2 * i)
            return carry

        lax.fori_loop(edge, pairs - edge, interior, 0, unroll=2)

    def over_edge(body, side):
        start = 0 if side == 0 else pairs - edge

        def one(i, carry):
            body(2 * i)
            return carry

        lax.fori_loop(start, start + edge, one, 0, unroll=2)

    def first_stiff(x):
        for p, part in enumerate(stiff_pair(x)):
            ku0[x + p] = part + stencil(u_a, x + p)

    load_coeffs.wait()
    over_interior(first_stiff)
    for side in range(2):
        take_halo(0, side, u_a)
        over_edge(first_stiff, side)
    f_in[2 * nb] = jnp.zeros(f_in.shape[1:], BF16)
    own_copy.wait()
    load_back.wait()
    load_prev.wait()
    for c in fetches:
        c.wait()

    def take_tile(i, carry):
        for q in range(tiles_y):
            tiles[i * tiles_y + q] = f_in[own_sm[0, q * planes + i]]
        return carry

    lax.fori_loop(0, planes, take_tile, 0, unroll=2)

    def speed_pair(x):
        blocks = tiles[pl.ds(x * tiles_y, 2 * tiles_y)].reshape(2 * half_rows, LANES)
        high, low = split(dot(blocks, interp_z[...]))
        right = jnp.concatenate(
            [
                jnp.concatenate([high[:half_rows], high[half_rows:]], axis=1),
                jnp.concatenate([low[:half_rows], low[half_rows:]], axis=1),
            ],
            axis=0,
        )
        perturb = dot(w_fwd[...], right)
        for p in range(2):
            speed[x + p] = speed[x + p] * jnp.exp(perturb[:, p * LANES : (p + 1) * LANES])

    def advance(x, force, step, now, prev):
        change = speed[x] * force
        drawn = adj[step, x] * change
        if step == steps - 1:
            ku0[x] = change
            u_hl[x, 1] = (kern[x] - drawn).astype(BF16)
            return
        if step == 0:
            kern[x] = -drawn
        else:
            kern[x] = kern[x] - drawn
        later = 2.0 * now[x + reach] - prev[x + reach] - change
        prev[x + reach] = later
        high, low = split(later)
        u_hl[x, 0] = high
        u_hl[x, 1] = low

    load_adj[0].wait()

    def first_step(x):
        speed_pair(x)
        for p in range(2):
            advance(x + p, ku0[x + p], 0, u_a, u_b)

    for side in range(2):
        over_edge(first_step, side)
        send_halo(1, side)
    over_interior(first_step)
    now, prev = u_b, u_a
    for step in range(1, steps):
        load_adj[step].wait()

        def body(x):
            parts = stiff_pair(x)
            for p in range(2):
                advance(x + p, parts[p] + stencil(now, x + p), step, now, prev)

        over_interior(body)
        for i in range(2):
            side = (step + i) % 2
            take_halo(step, side, now)
            over_edge(body, side)
            if step < steps - 1:
                send_halo(step + 1, side)
        now, prev = prev, now
    now, prev = prev, now

    def grad_pair(i, carry):
        x = 2 * i
        right = jnp.concatenate([u_hl[x, 1], u_hl[x + 1, 1]], axis=1)
        back = dot(w_bwd[...], right)
        parts = []
        for p in range(2):
            high, low = split(back[:, p * LANES : (p + 1) * LANES])
            parts.append(jnp.concatenate([high, low], axis=1))
        grads = dot(jnp.concatenate(parts, axis=0), w_iz[...])
        g_tiles[pl.ds(x * tiles_y, 2 * tiles_y)] = grads.astype(BF16).reshape(
            2 * tiles_y, rows_b, LANES
        )
        return carry

    lax.fori_loop(0, pairs, grad_pair, 0, unroll=4)
    g_tiles[n_tiles] = jnp.zeros(g_tiles.shape[1:], BF16)

    def pack(i, carry):
        for j in range(ne):
            g_a[j, i] = g_tiles[own_sm[1, j * ns + i]]
            g_b[i, j] = g_tiles[own_sm[2, j * ns + i]]
        return carry

    lax.fori_loop(0, ns, pack, 0)
    begin, middle, end = exchange(
        g_a,
        g_b,
        g_ra,
        g_rb,
        g_in,
        (ga1_send, ga1_recv, ga2_send, ga2_recv, gb1_send, gb1_recv, gb2_send, gb2_recv),
        g_loc,
    )
    begin()

    def last_wave(i, carry):
        prev[reach + i] = 2.0 * now[reach + i] - prev[reach + i] - ku0[i]
        return carry

    lax.fori_loop(0, planes, last_wave, 0)
    wave_copy = pltpu.make_async_copy(prev.at[pl.ds(reach, planes)], wave_out.at[0], out_sem)
    wave_copy.start()
    middle()

    for c in ask_copies:
        c.wait()
    ranks = []
    for r in range(2):
        table = jnp.zeros((ROWS, LANES), I32)
        for i in range(ne):
            table = jnp.where(
                sub == i, jnp.broadcast_to(asked_all[i][r : r + 1], (ROWS, LANES)), table
            )
        ranks.append(table)
    width = ns * rows_b
    lane = iota((LANES, width), 1)
    pick = jnp.where(iota((LANES, width), 0) == lane // rows_b * ROWS + e, 1.0, 0.0)
    asked_both = jnp.concatenate(ranks, axis=0).astype(F32).astype(BF16)
    keys = dot(asked_both, pick.astype(BF16)).astype(I32) * rows_b
    keys = keys + iota((2 * ROWS, width), 1) % rows_b
    rows = iota((blk * rows_b, width), 0)
    for r in range(2):
        for i in range(ne):
            key = keys[r * ROWS + i : r * ROWS + i + 1]
            hot = jnp.where(jnp.broadcast_to(key, rows.shape) == rows, 1.0, 0.0)
            at = (r * ne + i) * width
            one_hot[:, at : at + width] = hot.astype(BF16)
    end()
    received = g_in[...].reshape(2 * nb * rows_b, LANES)
    total = dot(one_hot[...], received)
    grad_out[...] = total.reshape(grad_out.shape)
    wave_copy.wait()


def cfg_shift(blk):
    return blk.bit_length() - 1


def shards(
    wave_prev,
    wave_now,
    adjoint,
    background,
    coeffs_x,
    stiff_y,
    stiff_z,
    interp_y,
    interp_z,
    model,
    block_index,
    live_count,
):
    ne = lax.axis_size("event")
    ns = lax.axis_size("slab")
    nb = ne * ns
    blk, rows_b, _ = model.shape
    planes, ny, nz = wave_now.shape[1:]
    steps = adjoint.shape[1]
    reach = (coeffs_x.shape[2] - 1) // 2
    tiles_y = block_index.shape[2]
    n_tiles = planes * tiles_y
    rows_t = ny // tiles_y
    ids = jnp.swapaxes(block_index, 1, 2)
    coeffs = jnp.transpose(coeffs_x, (2, 0, 1))
    cfg = (ne, ns, planes, reach, steps, n_tiles, rows_t, blk, rows_b)
    dma = pltpu.SemaphoreType.DMA
    vmem = pltpu.VMEM
    slot = (rows_b, nz)

    def buffers():
        return [
            vmem((ne, ns) + slot, BF16),
            vmem((ns, ne) + slot, BF16),
            vmem((ne, ns) + slot, BF16),
            vmem((ns, ne) + slot, BF16),
        ]

    def sems():
        return [dma((n,)) for n in (ne, ne, ns, ns, ns, ns, ne, ne)] + [dma((4,))]

    grads = buffers()
    whole = pl.BlockSpec(memory_space=pltpu.VMEM)
    smem = pl.BlockSpec(memory_space=pltpu.SMEM)
    hbm = pl.BlockSpec(memory_space=pl.ANY)
    wave, grad = pl.pallas_call(
        functools.partial(window_kernel, cfg),
        out_shape=(
            jax.ShapeDtypeStruct(wave_now.shape, F32),
            jax.ShapeDtypeStruct(model.shape, F32),
        ),
        in_specs=[hbm] * 5 + [smem] + [whole] * 6,
        out_specs=(hbm, whole),
        scratch_shapes=[
            vmem((planes + 2 * reach, ny, nz), F32),
            vmem((planes + 2 * reach, ny, nz), F32),
            vmem((planes, 2, ny, nz), BF16),
            vmem((planes, ny, nz), F32),
            vmem((planes, ny, nz), F32),
            vmem((steps, planes, ny, nz), F32),
            vmem((planes, ny, nz), F32),
            vmem((steps, 2, reach, ny, nz), BF16),
            vmem((2 * ny, 2 * ny), BF16),
            vmem((2 * nz, 2 * nz), BF16),
            vmem((ny, 2 * tiles_y * rows_b), BF16),
            vmem((tiles_y * rows_b, ny), BF16),
            vmem((2 * nz, nz), BF16),
            pltpu.SMEM(coeffs.shape, F32),
            vmem((ROWS, LANES), I32),
            vmem((LANES // ROWS, ROWS, LANES), I32),
            vmem((ROWS, LANES), I32),
            vmem((ROWS, LANES), I32),
            vmem((ne, ROWS, LANES), I32),
            pltpu.SMEM((ROWS, LANES), I32),
            pltpu.SMEM((ROWS, LANES), I32),
            vmem((ne,) + model.shape, BF16),
            vmem((ns, 2 * ne) + slot, BF16),
            vmem((2 * nb + 1,) + slot, BF16),
            vmem((n_tiles,) + slot, BF16),
            vmem((n_tiles + 1,) + slot, BF16),
            *grads,
            vmem((2, ne, ns) + slot, BF16),
            vmem((blk * rows_b, 2 * nb * rows_b), BF16),
            dma((3 + steps,)),
            dma((3,)),
            dma((ns,)),
            dma((ns,)),
            dma((ne,)),
            dma((ne,)),
            dma((ne,)),
            dma((ne,)),
            dma((ns,)),
            dma((ns,)),
            dma((steps, 2)),
            dma((steps, 2)),
            dma,
            *sems(),
            dma,
        ],
        compiler_params=pltpu.CompilerParams(
            collective_id=0, has_side_effects=True, vmem_limit_bytes=56 * 1024 * 1024
        ),
        name="window",
    )(
        wave_prev,
        wave_now,
        adjoint,
        background,
        coeffs,
        live_count,
        stiff_y,
        stiff_z,
        interp_y,
        interp_z,
        model,
        ids,
    )
    return wave, grad


def solution(mesh):
    return jax.shard_map(
        shards,
        mesh=mesh,
        in_specs=(
            P("event", "slab", None, None),
            P("event", "slab", None, None),
            P("event", None, "slab", None, None),
            P("event", "slab", None, None),
            P("event", "slab", None),
            P(),
            P(),
            P(),
            P(),
            P(("event", "slab"), None, None),
            P("event", "slab", None),
            P("event", "slab"),
        ),
        out_specs=(P("event", "slab", None, None), P(("event", "slab"), None, None)),
        check_vma=False,
    )
```

```python
import functools
import math

import jax
import jax.numpy as jnp
from jax import lax
from jax.experimental import pallas as pl
from jax.experimental.pallas import tpu as pltpu
from jax.sharding import PartitionSpec as P

F32 = jnp.float32
BF16 = jnp.bfloat16
I32 = jnp.int32
MESH = pl.DeviceIdType.MESH
ROWS = 8
LANES = 128


def split(value):
    high = value.astype(BF16)
    low = (value - high.astype(F32)).astype(BF16)
    return high, low


def iota(shape, dim):
    return lax.broadcasted_iota(I32, shape, dim)


def dot(a, b):
    return jnp.dot(a, b, preferred_element_type=F32)


def window_kernel(
    cfg,
    prev_hbm,
    now_hbm,
    adj_hbm,
    back_hbm,
    coeffs_hbm,
    live,
    stiff_y_hbm,
    stiff_z_hbm,
    interp_y_hbm,
    interp_z_hbm,
    model,
    ids_hbm,
    wave_out,
    grad_out,
    u_a,
    u_b,
    u_hl,
    speed,
    kern,
    adj,
    ku0,
    halo,
    w_y,
    w_z,
    w_fwd,
    w_bwd,
    w_iz,
    coeffs,
    stiff_y,
    stiff_z,
    interp_y,
    interp_z,
    ids_in,
    id_own,
    id_all,
    idx_own,
    idx_req,
    asked_all,
    own_sm,
    req_sm,
    column,
    f_out,
    f_in,
    tiles,
    g_tiles,
    g_a,
    g_b,
    g_ra,
    g_rb,
    g_in,
    one_hot,
    load_sem,
    small_sem,
    idx_sem,
    id_send,
    id_recv,
    col_send,
    col_recv,
    pair_send,
    pair_recv,
    ask_send,
    ask_recv,
    f_send,
    f_recv,
    h_send,
    h_recv,
    f_loc,
    ga1_send,
    ga1_recv,
    ga2_send,
    ga2_recv,
    gb1_send,
    gb1_recv,
    gb2_send,
    gb2_recv,
    g_loc,
    out_sem,
):
    ne, ns, planes, reach, steps, n_tiles, rows_t, blk, rows_b = cfg
    nb = ne * ns
    e = lax.axis_index("event")
    s = lax.axis_index("slab")
    tiles_y = LANES // rows_t

    load_now = pltpu.make_async_copy(now_hbm.at[0], u_a.at[pl.ds(reach, planes)], load_sem.at[0])
    load_prev = pltpu.make_async_copy(prev_hbm.at[0], u_b.at[pl.ds(reach, planes)], load_sem.at[1])
    load_back = pltpu.make_async_copy(back_hbm.at[0], speed, load_sem.at[2])
    load_adj = [
        pltpu.make_async_copy(adj_hbm.at[0, i], adj.at[i], load_sem.at[3 + i]) for i in range(steps)
    ]
    load_coeffs = pltpu.make_async_copy(coeffs_hbm, coeffs, idx_sem.at[2])
    load_ids = pltpu.make_async_copy(ids_hbm, ids_in, small_sem.at[0])
    load_model = pltpu.make_async_copy(model, column.at[e], small_sem.at[1])
    load_weights = [
        pltpu.make_async_copy(stiff_y_hbm, stiff_y, small_sem.at[2]),
        pltpu.make_async_copy(stiff_z_hbm, stiff_z, small_sem.at[3]),
        pltpu.make_async_copy(interp_y_hbm, interp_y, small_sem.at[4]),
        pltpu.make_async_copy(interp_z_hbm, interp_z, small_sem.at[5]),
    ]
    load_ids.start()
    load_model.start()

    nz = ne // 2
    side_len = math.isqrt(ns)
    z, core = e // 2, lax.rem(e, 2)
    row, col = s // side_len, lax.rem(s, side_len)

    def event_at(d):
        return lax.rem(z + d // 2, nz) * 2 + lax.rem(core + d % 2, 2)

    def slab_at(d):
        y = lax.rem(row + d // side_len, side_len)
        return y * side_len + lax.rem(col + d % side_len, side_len)

    def around(d, n):
        return min(d, n - d)

    event_order = sorted(range(1, ne), key=lambda d: -around(d // 2, nz))
    slab_order = sorted(
        range(1, ns),
        key=lambda d: -around(d // side_len, side_len) - around(d % side_len, side_len),
    )

    barrier = pltpu.get_barrier_semaphore()
    for d in slab_order:
        pl.semaphore_signal(barrier, inc=1, device_id=(e, slab_at(d)), device_id_type=MESH)
    for d in event_order:
        pl.semaphore_signal(barrier, inc=1, device_id=(event_at(d), s), device_id_type=MESH)
    load_now.start()
    for c in load_weights:
        c.start()
    load_coeffs.start()
    load_back.start()
    load_prev.start()

    def event_copy(src, dst, send, recv, d, at=None):
        at = d if at is None else at
        return pltpu.make_async_remote_copy(
            src_ref=src,
            dst_ref=dst,
            send_sem=send.at[at],
            recv_sem=recv.at[at],
            device_id=(event_at(d), s),
            device_id_type=MESH,
        )

    def slab_copy(src, dst, send, recv, d):
        return pltpu.make_async_remote_copy(
            src_ref=src,
            dst_ref=dst,
            send_sem=send.at[d],
            recv_sem=recv.at[d],
            device_id=(e, slab_at(d)),
            device_id_type=MESH,
        )

    far = [
        event_copy(column.at[e], column.at[e], col_send, col_recv, 2 * d) for d in range(1, nz)
    ]
    mine = [event_at(2 * ((nz - d) % nz)) for d in range(nz)]
    near = [
        event_copy(column.at[mine[d]], column.at[mine[d]], pair_send, pair_recv, 1, d)
        for d in range(nz)
    ]
    load_ids.wait()
    sub = iota((ROWS, LANES), 0)
    planes_id = ids_in[0]
    ids_row = jnp.concatenate([planes_id[q : q + 1] for q in range(tiles_y)], axis=1)
    if n_tiles < LANES:
        ids_row = jnp.concatenate([ids_row, jnp.full((1, LANES - n_tiles), -1, I32)], axis=1)
    ids = jnp.broadcast_to(ids_row, (ROWS, LANES))
    id_own[...] = ids
    for i in range(LANES // ROWS):
        if i >= ns:
            id_all[i] = jnp.full((ROWS, LANES), -1, I32)
    id_all[s] = ids
    pl.semaphore_wait(barrier, ne - 1 + ns - 1)
    id_copies = [slab_copy(id_own, id_all.at[s], id_send, id_recv, d) for d in slab_order]
    for c in id_copies:
        c.start()
    load_model.wait()
    for c in far[::-1]:
        c.start()
    near[0].start()
    for c in load_adj:
        c.start()

    owners = lax.shift_right_arithmetic(jnp.broadcast_to(ids_row, (LANES, LANES)), cfg_shift(blk))
    owners_t = jnp.transpose(owners)
    row_i = iota((LANES, LANES), 0)
    lane_i = iota((LANES, LANES), 1)
    earlier = jnp.where((owners == owners_t) & (row_i < lane_i), 1, 0)
    rank = jnp.sum(earlier, axis=0, keepdims=True)
    owner_row = owners[0:1]
    at_e = owner_row // ns
    at_s = owner_row - at_e * ns
    live_n = live[0, 0]

    def in_order(lane):
        return lane % planes * tiles_y + lane // planes

    address = at_s * (2 * ne) + rank * ne + at_e
    alive = in_order(iota((1, LANES), 1)) < live_n
    address = jnp.where(alive, address, 2 * nb)
    none = LANES
    match = owners == row_i
    first = jnp.min(jnp.where(match, lane_i, none), axis=1, keepdims=True)
    second = jnp.min(jnp.where(match & (lane_i > first), lane_i, none), axis=1, keepdims=True)

    def as_row(values):
        return jnp.transpose(jnp.broadcast_to(values, (LANES, LANES)))[0:1]

    def tile_at(lane):
        tile = in_order(lane)
        return jnp.where((lane < none) & (tile < live_n), tile, n_tiles)

    tile_0 = tile_at(as_row(first))
    tile_1 = tile_at(as_row(second))
    idx_own[...] = jnp.where(
        sub == 0,
        jnp.broadcast_to(address, (ROWS, LANES)),
        jnp.where(
            sub == 1,
            jnp.broadcast_to(tile_0, (ROWS, LANES)),
            jnp.broadcast_to(tile_1, (ROWS, LANES)),
        ),
    )
    own_copy = pltpu.make_async_copy(idx_own, own_sm, idx_sem.at[0])
    own_copy.start()

    for c in load_weights:
        c.wait()
    high, low = split(stiff_y[...])
    w_y[...] = jnp.concatenate(
        [jnp.concatenate([high, high], axis=1), jnp.concatenate([low, low], axis=1)], axis=0
    )
    high, low = split(jnp.transpose(stiff_z[...]))
    half = jnp.concatenate([high, low], axis=1)
    w_z[...] = jnp.concatenate([half, half], axis=0)

    load_now.wait()

    def split_planes(i, carry):
        high, low = split(u_a[reach + i])
        u_hl[i, 0] = high
        u_hl[i, 1] = low
        return carry

    def halo_copy(step, side):
        start = 0 if side == 0 else planes - reach
        return pltpu.make_async_remote_copy(
            src_ref=u_hl.at[pl.ds(start, reach), 0],
            dst_ref=halo.at[step, side],
            send_sem=h_send.at[step, side],
            recv_sem=h_recv.at[step, side],
            device_id=(e, lax.rem(s + (ns - 1 if side == 0 else 1), ns)),
            device_id_type=MESH,
        )

    def send_halo(step, side):
        @pl.when(s > 0 if side == 0 else s < ns - 1)
        def _():
            halo_copy(step, side).start()

    def take_halo(step, side, buf):
        @pl.when(s > 0 if side == 0 else s < ns - 1)
        def _():
            halo_copy(step, side).wait_send()
            halo_copy(step, 1 - side).wait_recv()
            at = 0 if side == 0 else reach + planes
            buf[pl.ds(at, reach)] = halo[step, 1 - side].astype(F32)

    lax.fori_loop(0, reach, split_planes, 0, unroll=2)
    lax.fori_loop(planes - reach, planes, split_planes, 0, unroll=2)
    send_halo(0, 0)
    send_halo(0, 1)
    for d in range(1, nz):
        far[d - 1].wait_recv()
        near[d].start()
    lax.fori_loop(reach, planes - reach, split_planes, 0, unroll=2)
    zero_halo = jnp.zeros((reach,) + u_a.shape[1:], F32)
    for buf in (u_a, u_b):
        buf[pl.ds(0, reach)] = zero_halo
        buf[pl.ds(reach + planes, reach)] = zero_halo

    for c in id_copies:
        c.wait_recv()
    asked_ids = id_all[...].reshape(LANES, LANES)
    wanted = (row_i % ROWS) * ns + s
    asks = (lax.shift_right_arithmetic(asked_ids, cfg_shift(blk)) == wanted) & (row_i % ROWS < ne)
    code = lane_i * blk + (asked_ids & (blk - 1))
    none = LANES * blk
    code_0 = jnp.min(jnp.where(asks, code, none), axis=1, keepdims=True)
    code_1 = jnp.min(jnp.where(asks & (code > code_0), code, none), axis=1, keepdims=True)
    asked_0 = as_row(code_0) & (blk - 1)
    asked_1 = as_row(code_1) & (blk - 1)
    asked = jnp.where(
        sub == 0,
        jnp.broadcast_to(asked_0, (ROWS, LANES)),
        jnp.broadcast_to(asked_1, (ROWS, LANES)),
    )
    idx_req[...] = asked
    req_copy = pltpu.make_async_copy(idx_req, req_sm, idx_sem.at[1])
    req_copy.start()
    asked_all[e] = asked
    for c in near:
        c.wait_recv()
    req_copy.wait()
    fetches = []
    for d in slab_order + [0]:
        to = slab_at(d)
        for j in range(ne):
            f_out[to, j] = column[j, req_sm[0, to * ROWS + j]]
            f_out[to, ne + j] = column[j, req_sm[1, to * ROWS + j]]
        dst = f_in.at[pl.ds(s * (2 * ne), 2 * ne)]
        if d == 0:
            c = pltpu.make_async_copy(f_out.at[to], dst, f_loc)
        else:
            c = slab_copy(f_out.at[to], dst, f_send, f_recv, d)
        c.start()
        fetches.append(c)
    ask_copies = [
        event_copy(idx_req, asked_all.at[e], ask_send, ask_recv, d) for d in event_order
    ]
    for c in ask_copies:
        c.start()
    for c in id_copies + far + near:
        c.wait_send()

    half_rows = tiles_y * rows_b
    pick_b = jnp.where(iota((half_rows, rows_b), 0) % rows_b == iota((half_rows, rows_b), 1), 1.0, 0.0)
    pick_y = jnp.where(iota((rows_t, LANES), 1) % rows_t == iota((rows_t, LANES), 0), 1.0, 0.0)
    wide = dot(pick_b.astype(BF16), interp_y[...]).astype(BF16)
    wide = dot(wide, pick_y.astype(BF16))
    on_diag = iota((half_rows, LANES), 0) // rows_b == iota((half_rows, LANES), 1) // rows_t
    diag = jnp.where(on_diag, wide, 0.0)
    w_bwd[...] = diag.astype(BF16)
    w_fwd[...] = jnp.transpose(jnp.concatenate([diag, diag], axis=0)).astype(BF16)
    iz_t = jnp.transpose(interp_z[...].astype(F32)).astype(BF16)
    w_iz[...] = jnp.concatenate([iz_t, iz_t], axis=0)

    ny = LANES

    def stiff_pair(x):
        a, b = u_hl[x, 0], u_hl[x, 1]
        c, d = u_hl[x + 1, 0], u_hl[x + 1, 1]
        left = jnp.concatenate(
            [jnp.concatenate([a, b], axis=1), jnp.concatenate([c, d], axis=1)], axis=0
        )
        right = jnp.concatenate(
            [jnp.concatenate([a, c], axis=1), jnp.concatenate([b, d], axis=1)], axis=0
        )
        along_z = dot(left, w_z[...])
        along_z = along_z[:, :LANES] + along_z[:, LANES:]
        along_y = dot(w_y[...], right)
        along_y = along_y[:ny] + along_y[ny:]
        return along_z[:ny] + along_y[:, :LANES], along_z[ny:] + along_y[:, LANES:]

    def stencil(buf, x):
        total = coeffs[0, 0, x] * buf[x]
        for k in range(1, 2 * reach + 1):
            total = total + coeffs[k, 0, x] * buf[x + k]
        return total

    pairs = planes // 2
    edge = reach // 2

    def over_interior(body):
        def interior(i, carry):
            body(2 * i)
            return carry

        lax.fori_loop(edge, pairs - edge, interior, 0, unroll=2)

    def over_edge(body, side):
        start = 0 if side == 0 else pairs - edge

        def one(i, carry):
            body(2 * i)
            return carry

        lax.fori_loop(start, start + edge, one, 0, unroll=2)

    def first_stiff(x):
        for p, part in enumerate(stiff_pair(x)):
            ku0[x + p] = part + stencil(u_a, x + p)

    load_coeffs.wait()
    over_interior(first_stiff)
    for side in range(2):
        take_halo(0, side, u_a)
        over_edge(first_stiff, side)
    f_in[2 * nb] = jnp.zeros(f_in.shape[1:], BF16)
    own_copy.wait()
    load_back.wait()
    load_prev.wait()
    for c in fetches[:-1]:
        c.wait_recv()
    for c in fetches[:-1]:
        c.wait_send()
    fetches[-1].wait()

    def take_tile(i, carry):
        for q in range(tiles_y):
            tiles[i * tiles_y + q] = f_in[own_sm[0, q * planes + i]]
        return carry

    lax.fori_loop(0, planes, take_tile, 0, unroll=2)

    def speed_pair(x):
        blocks = tiles[pl.ds(x * tiles_y, 2 * tiles_y)].reshape(2 * half_rows, LANES)
        high, low = split(dot(blocks, interp_z[...]))
        right = jnp.concatenate(
            [
                jnp.concatenate([high[:half_rows], high[half_rows:]], axis=1),
                jnp.concatenate([low[:half_rows], low[half_rows:]], axis=1),
            ],
            axis=0,
        )
        perturb = dot(w_fwd[...], right)
        for p in range(2):
            speed[x + p] = speed[x + p] * jnp.exp(perturb[:, p * LANES : (p + 1) * LANES])

    def advance(x, force, step, now, prev):
        change = speed[x] * force
        drawn = adj[step, x] * change
        if step == steps - 1:
            ku0[x] = change
            u_hl[x, 1] = (kern[x] - drawn).astype(BF16)
            return
        if step == 0:
            kern[x] = -drawn
        else:
            kern[x] = kern[x] - drawn
        later = 2.0 * now[x + reach] - prev[x + reach] - change
        prev[x + reach] = later
        high, low = split(later)
        u_hl[x, 0] = high
        u_hl[x, 1] = low

    load_adj[0].wait()

    def first_step(x):
        speed_pair(x)
        for p in range(2):
            advance(x + p, ku0[x + p], 0, u_a, u_b)

    for side in range(2):
        over_edge(first_step, side)
        send_halo(1, side)
    over_interior(first_step)
    now, prev = u_b, u_a
    for step in range(1, steps):
        load_adj[step].wait()

        def body(x):
            parts = stiff_pair(x)
            for p in range(2):
                advance(x + p, parts[p] + stencil(now, x + p), step, now, prev)

        over_interior(body)
        for i in range(2):
            side = (step + i) % 2
            take_halo(step, side, now)
            over_edge(body, side)
            if step < steps - 1:
                send_halo(step + 1, side)
        now, prev = prev, now
    now, prev = prev, now

    def grad_pair(i, carry):
        x = 2 * i
        right = jnp.concatenate([u_hl[x, 1], u_hl[x + 1, 1]], axis=1)
        back = dot(w_bwd[...], right)
        parts = []
        for p in range(2):
            high, low = split(back[:, p * LANES : (p + 1) * LANES])
            parts.append(jnp.concatenate([high, low], axis=1))
        grads = dot(jnp.concatenate(parts, axis=0), w_iz[...])
        g_tiles[pl.ds(x * tiles_y, 2 * tiles_y)] = grads.astype(BF16).reshape(
            2 * tiles_y, rows_b, LANES
        )
        return carry

    lax.fori_loop(0, pairs, grad_pair, 0, unroll=4)
    g_tiles[n_tiles] = jnp.zeros(g_tiles.shape[1:], BF16)

    def pack_event(d):
        to = event_at(d)

        def one(i, carry):
            g_a[to, i] = g_tiles[own_sm[1, to * ns + i]]
            return carry

        lax.fori_loop(0, ns, one, 0, unroll=ns)
        if d == 0:
            return pltpu.make_async_copy(g_a.at[to], g_ra.at[e], g_loc.at[0])
        return event_copy(g_a.at[to], g_ra.at[e], ga1_send, ga1_recv, d)

    def pack_slab(d):
        to = slab_at(d)
        for j in range(ne):
            g_b[to, j] = g_tiles[own_sm[2, j * ns + to]]
        if d == 0:
            return pltpu.make_async_copy(g_b.at[to], g_rb.at[s], g_loc.at[1])
        return slab_copy(g_b.at[to], g_rb.at[s], gb1_send, gb1_recv, d)

    a1, b1 = [], []
    events, slabs = event_order + [0], slab_order + [0]
    for i in range(max(ne, ns // 2)):
        for d in slabs[2 * i : 2 * i + 2]:
            b1.append(pack_slab(d))
            b1[-1].start()
        for d in events[i : i + 1]:
            a1.append(pack_event(d))
            a1[-1].start()
    a2 = [
        slab_copy(g_ra.at[:, slab_at(d)], g_in.at[0, :, s], ga2_send, ga2_recv, d)
        for d in slab_order
    ] + [pltpu.make_async_copy(g_ra.at[:, s], g_in.at[0, :, s], g_loc.at[2])]
    b2 = [
        event_copy(g_rb.at[:, event_at(d)], g_in.at[1, e], gb2_send, gb2_recv, d)
        for d in event_order
    ] + [pltpu.make_async_copy(g_rb.at[:, e], g_in.at[1, e], g_loc.at[3])]

    def arrive(copies):
        for c in copies[:-1]:
            c.wait_recv()
        copies[-1].wait()

    def last_wave(i, carry):
        prev[reach + i] = 2.0 * now[reach + i] - prev[reach + i] - ku0[i]
        return carry

    lax.fori_loop(0, planes, last_wave, 0)
    wave_copy = pltpu.make_async_copy(prev.at[pl.ds(reach, planes)], wave_out.at[0], out_sem)
    wave_copy.start()
    arrive(a1)
    for c in a2:
        c.start()
    arrive(b1)
    for c in b2:
        c.start()

    for c in ask_copies:
        c.wait_recv()
    ranks = []
    for r in range(2):
        table = jnp.zeros((ROWS, LANES), I32)
        for i in range(ne):
            table = jnp.where(
                sub == i, jnp.broadcast_to(asked_all[i][r : r + 1], (ROWS, LANES)), table
            )
        ranks.append(table)
    width = ns * rows_b
    lane = iota((LANES, width), 1)
    pick = jnp.where(iota((LANES, width), 0) == lane // rows_b * ROWS + e, 1.0, 0.0)
    asked_both = jnp.concatenate(ranks, axis=0).astype(F32).astype(BF16)
    keys = dot(asked_both, pick.astype(BF16)).astype(I32) * rows_b
    keys = keys + iota((2 * ROWS, width), 1) % rows_b
    rows = iota((blk * rows_b, width), 0)
    for r in range(2):
        for i in range(ne):
            key = keys[r * ROWS + i : r * ROWS + i + 1]
            hot = jnp.where(jnp.broadcast_to(key, rows.shape) == rows, 1.0, 0.0)
            at = (r * ne + i) * width
            one_hot[:, at : at + width] = hot.astype(BF16)
    half_slots = nb * rows_b
    arrive(a2)
    total = dot(one_hot[:, :half_slots], g_in[0].reshape(half_slots, LANES))
    arrive(b2)
    total = total + dot(one_hot[:, half_slots:], g_in[1].reshape(half_slots, LANES))
    grad_out[...] = total.reshape(grad_out.shape)
    for c in a1[:-1] + b1[:-1] + a2[:-1] + b2[:-1] + ask_copies:
        c.wait_send()
    wave_copy.wait()


def cfg_shift(blk):
    return blk.bit_length() - 1


def shards(
    wave_prev,
    wave_now,
    adjoint,
    background,
    coeffs_x,
    stiff_y,
    stiff_z,
    interp_y,
    interp_z,
    model,
    block_index,
    live_count,
):
    ne = lax.axis_size("event")
    ns = lax.axis_size("slab")
    nb = ne * ns
    blk, rows_b, _ = model.shape
    planes, ny, nz = wave_now.shape[1:]
    steps = adjoint.shape[1]
    reach = (coeffs_x.shape[2] - 1) // 2
    tiles_y = block_index.shape[2]
    n_tiles = planes * tiles_y
    rows_t = ny // tiles_y
    ids = jnp.swapaxes(block_index, 1, 2)
    coeffs = jnp.transpose(coeffs_x, (2, 0, 1))
    cfg = (ne, ns, planes, reach, steps, n_tiles, rows_t, blk, rows_b)
    arrays = (
        wave_prev,
        wave_now,
        adjoint,
        background,
        coeffs,
        live_count,
        stiff_y,
        stiff_z,
        interp_y,
        interp_z,
        model,
        ids,
    )
    arrays = [
        a if a is live_count else pltpu.with_memory_space_constraint(a, pltpu.HBM) for a in arrays
    ]
    dma = pltpu.SemaphoreType.DMA
    vmem = pltpu.VMEM
    slot = (rows_b, nz)

    def buffers():
        return [
            vmem((ne, ns) + slot, BF16),
            vmem((ns, ne) + slot, BF16),
            vmem((ne, ns) + slot, BF16),
            vmem((ns, ne) + slot, BF16),
        ]

    def sems():
        return [dma((n,)) for n in (ne, ne, ns, ns, ns, ns, ne, ne)] + [dma((4,))]

    grads = buffers()
    whole = pl.BlockSpec(memory_space=pltpu.VMEM)
    smem = pl.BlockSpec(memory_space=pltpu.SMEM)
    hbm = pl.BlockSpec(memory_space=pltpu.HBM)
    free = pl.BlockSpec(memory_space=pl.ANY)
    wave, grad = pl.pallas_call(
        functools.partial(window_kernel, cfg),
        out_shape=(
            jax.ShapeDtypeStruct(wave_now.shape, F32),
            jax.ShapeDtypeStruct(model.shape, F32),
        ),
        in_specs=[hbm] * 5 + [smem] + [hbm] * 6,
        out_specs=(free, whole),
        scratch_shapes=[
            vmem((planes + 2 * reach, ny, nz), F32),
            vmem((planes + 2 * reach, ny, nz), F32),
            vmem((planes, 2, ny, nz), BF16),
            vmem((planes, ny, nz), F32),
            vmem((planes, ny, nz), F32),
            vmem((steps, planes, ny, nz), F32),
            vmem((planes, ny, nz), F32),
            vmem((steps, 2, reach, ny, nz), BF16),
            vmem((2 * ny, 2 * ny), BF16),
            vmem((2 * nz, 2 * nz), BF16),
            vmem((ny, 2 * tiles_y * rows_b), BF16),
            vmem((tiles_y * rows_b, ny), BF16),
            vmem((2 * nz, nz), BF16),
            pltpu.SMEM(coeffs.shape, F32),
            vmem(stiff_y.shape, F32),
            vmem(stiff_z.shape, F32),
            vmem(interp_y.shape, BF16),
            vmem(interp_z.shape, BF16),
            vmem(ids.shape, I32),
            vmem((ROWS, LANES), I32),
            vmem((LANES // ROWS, ROWS, LANES), I32),
            vmem((ROWS, LANES), I32),
            vmem((ROWS, LANES), I32),
            vmem((ne, ROWS, LANES), I32),
            pltpu.SMEM((ROWS, LANES), I32),
            pltpu.SMEM((ROWS, LANES), I32),
            vmem((ne,) + model.shape, BF16),
            vmem((ns, 2 * ne) + slot, BF16),
            vmem((2 * nb + 1,) + slot, BF16),
            vmem((n_tiles,) + slot, BF16),
            vmem((n_tiles + 1,) + slot, BF16),
            *grads,
            vmem((2, ne, ns) + slot, BF16),
            vmem((blk * rows_b, 2 * nb * rows_b), BF16),
            dma((3 + steps,)),
            dma((6,)),
            dma((3,)),
            dma((ns,)),
            dma((ns,)),
            dma((ne,)),
            dma((ne,)),
            dma((ne // 2,)),
            dma((ne // 2,)),
            dma((ne,)),
            dma((ne,)),
            dma((ns,)),
            dma((ns,)),
            dma((steps, 2)),
            dma((steps, 2)),
            dma,
            *sems(),
            dma,
        ],
        compiler_params=pltpu.CompilerParams(
            collective_id=0, has_side_effects=True, vmem_limit_bytes=40 * 1024 * 1024
        ),
        name="window",
    )(*arrays)
    return wave, grad


def solution(mesh):
    return jax.shard_map(
        shards,
        mesh=mesh,
        in_specs=(
            P("event", "slab", None, None),
            P("event", "slab", None, None),
            P("event", None, "slab", None, None),
            P("event", "slab", None, None),
            P("event", "slab", None),
            P(),
            P(),
            P(),
            P(),
            P(("event", "slab"), None, None),
            P("event", "slab", None),
            P("event", "slab"),
        ),
        out_specs=(P("event", "slab", None, None), P(("event", "slab"), None, None)),
        check_vma=False,
    )
```

```python
import functools
import math

import jax
import jax.numpy as jnp
from jax import lax
from jax.experimental import pallas as pl
from jax.experimental.pallas import tpu as pltpu
from jax.sharding import PartitionSpec as P

F32 = jnp.float32
BF16 = jnp.bfloat16
I32 = jnp.int32
MESH = pl.DeviceIdType.MESH
ROWS = 8
LANES = 128


def split(value):
    high = value.astype(BF16)
    low = (value - high.astype(F32)).astype(BF16)
    return high, low


def iota(shape, dim):
    return lax.broadcasted_iota(I32, shape, dim)


def dot(a, b):
    return jnp.dot(a, b, preferred_element_type=F32)


def window_kernel(
    cfg,
    prev_hbm,
    now_hbm,
    adj_hbm,
    back_hbm,
    coeffs_hbm,
    live,
    stiff_y_hbm,
    stiff_z_hbm,
    interp_y_hbm,
    interp_z_hbm,
    model,
    ids_hbm,
    wave_out,
    grad_out,
    u_a,
    u_b,
    u_hl,
    speed,
    kern,
    adj,
    ku0,
    halo,
    w_y,
    w_z,
    w_fwd,
    w_bwd,
    w_iz,
    coeffs,
    stiff_y,
    stiff_z,
    interp_y,
    interp_z,
    ids_in,
    id_own,
    id_all,
    idx_own,
    idx_req,
    asked_all,
    own_sm,
    req_sm,
    column,
    f_out,
    f_in,
    g_tiles,
    g_a,
    g_b,
    g_ra,
    g_rb,
    g_in,
    one_hot,
    load_sem,
    small_sem,
    idx_sem,
    id_send,
    id_recv,
    col_send,
    col_recv,
    pair_send,
    pair_recv,
    ask_send,
    ask_recv,
    f_send,
    f_recv,
    h_send,
    h_recv,
    f_loc,
    ga1_send,
    ga1_recv,
    ga2_send,
    ga2_recv,
    gb1_send,
    gb1_recv,
    gb2_send,
    gb2_recv,
    g_loc,
    out_sem,
):
    ne, ns, planes, reach, steps, n_tiles, rows_t, blk, rows_b = cfg
    nb = ne * ns
    e = lax.axis_index("event")
    s = lax.axis_index("slab")
    tiles_y = LANES // rows_t

    load_now = pltpu.make_async_copy(now_hbm.at[0], u_a.at[pl.ds(reach, planes)], load_sem.at[0])
    load_prev = pltpu.make_async_copy(prev_hbm.at[0], u_b.at[pl.ds(reach, planes)], load_sem.at[1])
    load_back = pltpu.make_async_copy(back_hbm.at[0], speed, load_sem.at[2])
    load_adj = [
        pltpu.make_async_copy(adj_hbm.at[0, i], adj.at[i], load_sem.at[3 + i]) for i in range(steps)
    ]
    load_coeffs = pltpu.make_async_copy(coeffs_hbm, coeffs, idx_sem.at[2])
    load_ids = pltpu.make_async_copy(ids_hbm, ids_in, small_sem.at[0])
    load_model = pltpu.make_async_copy(model, column.at[e], small_sem.at[1])
    load_weights = [
        pltpu.make_async_copy(stiff_y_hbm, stiff_y, small_sem.at[2]),
        pltpu.make_async_copy(stiff_z_hbm, stiff_z, small_sem.at[3]),
        pltpu.make_async_copy(interp_y_hbm, interp_y, small_sem.at[4]),
        pltpu.make_async_copy(interp_z_hbm, interp_z, small_sem.at[5]),
    ]
    load_ids.start()
    load_model.start()

    nz = ne // 2
    side_len = math.isqrt(ns)
    z, core = e // 2, lax.rem(e, 2)
    row, col = s // side_len, lax.rem(s, side_len)

    def event_at(d):
        return lax.rem(z + d // 2, nz) * 2 + lax.rem(core + d % 2, 2)

    def slab_at(d):
        y = lax.rem(row + d // side_len, side_len)
        return y * side_len + lax.rem(col + d % side_len, side_len)

    def around(d, n):
        return min(d, n - d)

    event_order = sorted(range(1, ne), key=lambda d: -around(d // 2, nz))
    slab_order = sorted(
        range(1, ns),
        key=lambda d: -around(d // side_len, side_len) - around(d % side_len, side_len),
    )

    barrier = pltpu.get_barrier_semaphore()
    for d in slab_order:
        pl.semaphore_signal(barrier, inc=1, device_id=(e, slab_at(d)), device_id_type=MESH)
    for d in event_order:
        pl.semaphore_signal(barrier, inc=1, device_id=(event_at(d), s), device_id_type=MESH)
    load_now.start()
    for c in load_weights:
        c.start()
    load_coeffs.start()
    load_back.start()
    load_prev.start()

    def event_copy(src, dst, send, recv, d, at=None):
        at = d if at is None else at
        return pltpu.make_async_remote_copy(
            src_ref=src,
            dst_ref=dst,
            send_sem=send.at[at],
            recv_sem=recv.at[at],
            device_id=(event_at(d), s),
            device_id_type=MESH,
        )

    def slab_copy(src, dst, send, recv, d):
        return pltpu.make_async_remote_copy(
            src_ref=src,
            dst_ref=dst,
            send_sem=send.at[d],
            recv_sem=recv.at[d],
            device_id=(e, slab_at(d)),
            device_id_type=MESH,
        )

    far = [
        event_copy(column.at[e], column.at[e], col_send, col_recv, 2 * d) for d in range(1, nz)
    ]
    mine = [event_at(2 * ((nz - d) % nz)) for d in range(nz)]
    near = [
        event_copy(column.at[mine[d]], column.at[mine[d]], pair_send, pair_recv, 1, d)
        for d in range(nz)
    ]
    load_ids.wait()
    sub = iota((ROWS, LANES), 0)
    planes_id = ids_in[0]
    ids_row = jnp.concatenate([planes_id[q : q + 1] for q in range(tiles_y)], axis=1)
    if n_tiles < LANES:
        ids_row = jnp.concatenate([ids_row, jnp.full((1, LANES - n_tiles), -1, I32)], axis=1)
    ids = jnp.broadcast_to(ids_row, (ROWS, LANES))
    id_own[...] = ids
    for i in range(LANES // ROWS):
        if i >= ns:
            id_all[i] = jnp.full((ROWS, LANES), -1, I32)
    id_all[s] = ids
    pl.semaphore_wait(barrier, ne - 1 + ns - 1)
    id_copies = [slab_copy(id_own, id_all.at[s], id_send, id_recv, d) for d in slab_order]
    for c in id_copies:
        c.start()
    load_model.wait()
    for c in far[::-1]:
        c.start()
    near[0].start()
    for c in load_adj:
        c.start()

    owners = lax.shift_right_arithmetic(jnp.broadcast_to(ids_row, (LANES, LANES)), cfg_shift(blk))
    owners_t = jnp.transpose(owners)
    row_i = iota((LANES, LANES), 0)
    lane_i = iota((LANES, LANES), 1)
    earlier = jnp.where((owners == owners_t) & (row_i < lane_i), 1, 0)
    rank = jnp.sum(earlier, axis=0, keepdims=True)
    owner_row = owners[0:1]
    at_e = owner_row // ns
    at_s = owner_row - at_e * ns
    live_n = live[0, 0]

    def in_order(lane):
        return lane % planes * tiles_y + lane // planes

    address = at_s * (2 * ne) + rank * ne + at_e
    alive = in_order(iota((1, LANES), 1)) < live_n
    address = jnp.where(alive, address, 2 * nb)
    none = LANES
    match = owners == row_i
    first = jnp.min(jnp.where(match, lane_i, none), axis=1, keepdims=True)
    second = jnp.min(jnp.where(match & (lane_i > first), lane_i, none), axis=1, keepdims=True)

    def as_row(values):
        return jnp.transpose(jnp.broadcast_to(values, (LANES, LANES)))[0:1]

    def tile_at(lane):
        tile = in_order(lane)
        return jnp.where((lane < none) & (tile < live_n), tile, n_tiles)

    tile_0 = tile_at(as_row(first))
    tile_1 = tile_at(as_row(second))
    idx_own[...] = jnp.where(
        sub == 0,
        jnp.broadcast_to(address, (ROWS, LANES)),
        jnp.where(
            sub == 1,
            jnp.broadcast_to(tile_0, (ROWS, LANES)),
            jnp.broadcast_to(tile_1, (ROWS, LANES)),
        ),
    )
    own_copy = pltpu.make_async_copy(idx_own, own_sm, idx_sem.at[0])
    own_copy.start()

    for c in load_weights:
        c.wait()
    high, low = split(stiff_y[...])
    w_y[...] = jnp.concatenate(
        [jnp.concatenate([high, high], axis=1), jnp.concatenate([low, low], axis=1)], axis=0
    )
    high, low = split(jnp.transpose(stiff_z[...]))
    half = jnp.concatenate([high, low], axis=1)
    w_z[...] = jnp.concatenate([half, half], axis=0)

    load_now.wait()

    def split_planes(i, carry):
        high, low = split(u_a[reach + i])
        u_hl[i, 0] = high
        u_hl[i, 1] = low
        return carry

    def halo_copy(step, side):
        start = 0 if side == 0 else planes - reach
        return pltpu.make_async_remote_copy(
            src_ref=u_hl.at[pl.ds(start, reach), 0],
            dst_ref=halo.at[step, side],
            send_sem=h_send.at[step, side],
            recv_sem=h_recv.at[step, side],
            device_id=(e, lax.rem(s + (ns - 1 if side == 0 else 1), ns)),
            device_id_type=MESH,
        )

    def send_halo(step, side):
        @pl.when(s > 0 if side == 0 else s < ns - 1)
        def _():
            halo_copy(step, side).start()

    def take_halo(step, side):
        @pl.when(s > 0 if side == 0 else s < ns - 1)
        def _():
            halo_copy(step, side).wait_send()
            halo_copy(step, 1 - side).wait_recv()

    lax.fori_loop(0, reach, split_planes, 0, unroll=2)
    lax.fori_loop(planes - reach, planes, split_planes, 0, unroll=2)
    send_halo(0, 0)
    send_halo(0, 1)
    for d in range(1, nz):
        far[d - 1].wait_recv()
        near[d].start()
    lax.fori_loop(reach, planes - reach, split_planes, 0, unroll=2)
    for side in range(2):

        @pl.when(s == (0 if side == 0 else ns - 1))
        def _():
            halo[:, 1 - side] = jnp.zeros((steps, reach) + u_a.shape[1:], BF16)

    for c in id_copies:
        c.wait_recv()
    asked_ids = id_all[...].reshape(LANES, LANES)
    wanted = (row_i % ROWS) * ns + s
    asks = (lax.shift_right_arithmetic(asked_ids, cfg_shift(blk)) == wanted) & (row_i % ROWS < ne)
    code = lane_i * blk + (asked_ids & (blk - 1))
    none = LANES * blk
    code_0 = jnp.min(jnp.where(asks, code, none), axis=1, keepdims=True)
    code_1 = jnp.min(jnp.where(asks & (code > code_0), code, none), axis=1, keepdims=True)
    asked_0 = as_row(code_0) & (blk - 1)
    asked_1 = as_row(code_1) & (blk - 1)
    asked = jnp.where(
        sub == 0,
        jnp.broadcast_to(asked_0, (ROWS, LANES)),
        jnp.broadcast_to(asked_1, (ROWS, LANES)),
    )
    idx_req[...] = asked
    req_copy = pltpu.make_async_copy(idx_req, req_sm, idx_sem.at[1])
    req_copy.start()
    asked_all[e] = asked
    for c in near:
        c.wait_recv()
    req_copy.wait()
    fetches = []
    for d in slab_order + [0]:
        to = slab_at(d)
        for j in range(ne):
            f_out[to, j] = column[j, req_sm[0, to * ROWS + j]]
            f_out[to, ne + j] = column[j, req_sm[1, to * ROWS + j]]
        dst = f_in.at[pl.ds(s * (2 * ne), 2 * ne)]
        if d == 0:
            c = pltpu.make_async_copy(f_out.at[to], dst, f_loc)
        else:
            c = slab_copy(f_out.at[to], dst, f_send, f_recv, d)
        c.start()
        fetches.append(c)
    ask_copies = [
        event_copy(idx_req, asked_all.at[e], ask_send, ask_recv, d) for d in event_order
    ]
    for c in ask_copies:
        c.start()
    for c in id_copies + far + near:
        c.wait_send()

    half_rows = tiles_y * rows_b
    pick_b = jnp.where(iota((half_rows, rows_b), 0) % rows_b == iota((half_rows, rows_b), 1), 1.0, 0.0)
    pick_y = jnp.where(iota((rows_t, LANES), 1) % rows_t == iota((rows_t, LANES), 0), 1.0, 0.0)
    wide = dot(pick_b.astype(BF16), interp_y[...]).astype(BF16)
    wide = dot(wide, pick_y.astype(BF16))
    on_diag = iota((half_rows, LANES), 0) // rows_b == iota((half_rows, LANES), 1) // rows_t
    diag = jnp.where(on_diag, wide, 0.0)
    w_bwd[...] = diag.astype(BF16)
    w_fwd[...] = jnp.transpose(jnp.concatenate([diag, diag], axis=0)).astype(BF16)
    iz_t = jnp.transpose(interp_z[...].astype(F32)).astype(BF16)
    w_iz[...] = jnp.concatenate([iz_t, iz_t], axis=0)

    ny = LANES

    def stiff_pair(x):
        a, b = u_hl[x, 0], u_hl[x, 1]
        c, d = u_hl[x + 1, 0], u_hl[x + 1, 1]
        left = jnp.concatenate(
            [jnp.concatenate([a, b], axis=1), jnp.concatenate([c, d], axis=1)], axis=0
        )
        right = jnp.concatenate(
            [jnp.concatenate([a, c], axis=1), jnp.concatenate([b, d], axis=1)], axis=0
        )
        along_z = dot(left, w_z[...])
        along_z = along_z[:, :LANES] + along_z[:, LANES:]
        along_y = dot(w_y[...], right)
        along_y = along_y[:ny] + along_y[ny:]
        return along_z[:ny] + along_y[:, :LANES], along_z[ny:] + along_y[:, LANES:]

    def stencil(buf, x):
        total = coeffs[0, 0, x] * buf[x]
        for k in range(1, 2 * reach + 1):
            total = total + coeffs[k, 0, x] * buf[x + k]
        return total

    pairs = planes // 2
    edge = reach // 2

    def over_interior(body, unroll=2):
        def interior(i, carry):
            body(2 * i)
            return carry

        lax.fori_loop(edge, pairs - edge, interior, 0, unroll=unroll)

    def side_planes(side):
        return range(reach) if side == 0 else range(planes - reach, planes)

    def over_edge(body, side):
        start = 0 if side == 0 else pairs - edge

        def one(i, carry):
            body(2 * i)
            return carry

        lax.fori_loop(start, start + edge, one, 0, unroll=2)

    def own_part(buf, side):
        for x in side_planes(side)[::2]:
            for p, part in enumerate(stiff_pair(x)):
                total = part
                for k in range(2 * reach + 1):
                    if 0 <= x + p + k - reach < planes:
                        total = total + coeffs[k, 0, x + p] * buf[x + p + k]
                ku0[x + p] = total

    def whole_part(step, x):
        total = ku0[x]
        for k in range(2 * reach + 1):
            at = x + k - reach
            if at < 0:
                total = total + coeffs[k, 0, x] * halo[step, 1, at + reach].astype(F32)
            if at >= planes:
                total = total + coeffs[k, 0, x] * halo[step, 0, at - planes].astype(F32)
        return total

    def first_stiff(x):
        for p, part in enumerate(stiff_pair(x)):
            ku0[x + p] = part + stencil(u_a, x + p)

    load_coeffs.wait()
    over_interior(first_stiff)
    for side in range(2):
        own_part(u_a, side)
    for side in range(2):
        take_halo(0, side)
        for x in side_planes(side):
            ku0[x] = whole_part(0, x)
    f_in[2 * nb] = jnp.zeros(f_in.shape[1:], BF16)
    own_copy.wait()
    load_back.wait()
    load_prev.wait()
    for c in fetches[:-1]:
        c.wait_recv()
    for c in fetches[:-1]:
        c.wait_send()
    fetches[-1].wait()

    def speed_pair(x):
        blocks = jnp.concatenate(
            [f_in[own_sm[0, q * planes + x + p]] for p in range(2) for q in range(tiles_y)], axis=0
        )
        high, low = split(dot(blocks, interp_z[...]))
        right = jnp.concatenate(
            [
                jnp.concatenate([high[:half_rows], high[half_rows:]], axis=1),
                jnp.concatenate([low[:half_rows], low[half_rows:]], axis=1),
            ],
            axis=0,
        )
        perturb = dot(w_fwd[...], right)
        for p in range(2):
            speed[x + p] = speed[x + p] * jnp.exp(perturb[:, p * LANES : (p + 1) * LANES])

    def grad_pair(x):
        right = jnp.concatenate([u_hl[x, 1], u_hl[x + 1, 1]], axis=1)
        back = dot(w_bwd[...], right)
        parts = []
        for p in range(2):
            high, low = split(back[:, p * LANES : (p + 1) * LANES])
            parts.append(jnp.concatenate([high, low], axis=1))
        grads = dot(jnp.concatenate(parts, axis=0), w_iz[...])
        g_tiles[pl.ds(x * tiles_y, 2 * tiles_y)] = grads.astype(BF16).reshape(
            2 * tiles_y, rows_b, LANES
        )

    g_tiles[n_tiles] = jnp.zeros(g_tiles.shape[1:], BF16)

    def advance(x, force, step, now, prev):
        change = speed[x] * force
        drawn = adj[step, x] * change
        if step == steps - 1:
            ku0[x] = change
            u_hl[x, 1] = (kern[x] - drawn).astype(BF16)
            return
        if step == 0:
            kern[x] = -drawn
        else:
            kern[x] = kern[x] - drawn
        later = 2.0 * now[x + reach] - prev[x + reach] - change
        prev[x + reach] = later
        high, low = split(later)
        u_hl[x, 0] = high
        u_hl[x, 1] = low

    load_adj[0].wait()

    def first_step(x):
        speed_pair(x)
        for p in range(2):
            advance(x + p, ku0[x + p], 0, u_a, u_b)

    for side in range(2):
        over_edge(first_step, side)
        send_halo(1, side)
    over_interior(first_step)
    now, prev = u_b, u_a
    for step in range(1, steps):
        load_adj[step].wait()

        def body(x):
            parts = stiff_pair(x)
            for p in range(2):
                advance(x + p, parts[p] + stencil(now, x + p), step, now, prev)

        over_interior(body)
        for side in range(2):
            own_part(now, side)
        last = step == steps - 1
        if last:
            over_interior(grad_pair, 4)
        for i in range(2):
            side = (step + i) % 2
            take_halo(step, side)
            for x in side_planes(side):
                advance(x, whole_part(step, x), step, now, prev)
            if last:
                over_edge(grad_pair, side)
            else:
                send_halo(step + 1, side)
        now, prev = prev, now
    now, prev = prev, now

    def pack_event(d):
        to = event_at(d)

        def one(i, carry):
            g_a[to, i] = g_tiles[own_sm[1, to * ns + i]]
            return carry

        lax.fori_loop(0, ns, one, 0, unroll=ns)
        if d == 0:
            return pltpu.make_async_copy(g_a.at[to], g_ra.at[e], g_loc.at[0])
        return event_copy(g_a.at[to], g_ra.at[e], ga1_send, ga1_recv, d)

    def pack_slab(d):
        to = slab_at(d)
        for j in range(ne):
            g_b[to, j] = g_tiles[own_sm[2, j * ns + to]]
        if d == 0:
            return pltpu.make_async_copy(g_b.at[to], g_rb.at[s], g_loc.at[1])
        return slab_copy(g_b.at[to], g_rb.at[s], gb1_send, gb1_recv, d)

    a1, b1 = [], []
    events, slabs = event_order + [0], slab_order + [0]
    for i in range(max(ne, ns // 2)):
        for d in slabs[2 * i : 2 * i + 2]:
            b1.append(pack_slab(d))
            b1[-1].start()
        for d in events[i : i + 1]:
            a1.append(pack_event(d))
            a1[-1].start()
    a2 = [
        slab_copy(g_ra.at[:, slab_at(d)], g_in.at[0, :, s], ga2_send, ga2_recv, d)
        for d in slab_order
    ] + [pltpu.make_async_copy(g_ra.at[:, s], g_in.at[0, :, s], g_loc.at[2])]
    b2 = [
        event_copy(g_rb.at[:, event_at(d)], g_in.at[1, e], gb2_send, gb2_recv, d)
        for d in event_order
    ] + [pltpu.make_async_copy(g_rb.at[:, e], g_in.at[1, e], g_loc.at[3])]

    def arrive(copies):
        for c in copies[:-1]:
            c.wait_recv()
        copies[-1].wait()

    def last_wave(i, carry):
        prev[reach + i] = 2.0 * now[reach + i] - prev[reach + i] - ku0[i]
        return carry

    lax.fori_loop(0, planes, last_wave, 0)
    wave_copy = pltpu.make_async_copy(prev.at[pl.ds(reach, planes)], wave_out.at[0], out_sem)
    wave_copy.start()
    arrive(a1)
    for c in a2:
        c.start()
    arrive(b1)
    for c in b2:
        c.start()

    for c in ask_copies:
        c.wait_recv()
    ranks = []
    for r in range(2):
        table = jnp.zeros((ROWS, LANES), I32)
        for i in range(ne):
            table = jnp.where(
                sub == i, jnp.broadcast_to(asked_all[i][r : r + 1], (ROWS, LANES)), table
            )
        ranks.append(table)
    width = ns * rows_b
    lane = iota((LANES, width), 1)
    pick = jnp.where(iota((LANES, width), 0) == lane // rows_b * ROWS + e, 1.0, 0.0)
    asked_both = jnp.concatenate(ranks, axis=0).astype(F32).astype(BF16)
    keys = dot(asked_both, pick.astype(BF16)).astype(I32) * rows_b
    keys = keys + iota((2 * ROWS, width), 1) % rows_b
    rows = iota((blk * rows_b, width), 0)
    for r in range(2):
        for i in range(ne):
            key = keys[r * ROWS + i : r * ROWS + i + 1]
            hot = jnp.where(jnp.broadcast_to(key, rows.shape) == rows, 1.0, 0.0)
            at = (r * ne + i) * width
            one_hot[:, at : at + width] = hot.astype(BF16)
    half_slots = nb * rows_b
    arrive(a2)
    total = dot(one_hot[:, :half_slots], g_in[0].reshape(half_slots, LANES))
    arrive(b2)
    total = total + dot(one_hot[:, half_slots:], g_in[1].reshape(half_slots, LANES))
    grad_out[...] = total.reshape(grad_out.shape)
    for c in a1[:-1] + b1[:-1] + a2[:-1] + b2[:-1] + ask_copies:
        c.wait_send()
    wave_copy.wait()


def cfg_shift(blk):
    return blk.bit_length() - 1


def shards(
    wave_prev,
    wave_now,
    adjoint,
    background,
    coeffs_x,
    stiff_y,
    stiff_z,
    interp_y,
    interp_z,
    model,
    block_index,
    live_count,
):
    ne = lax.axis_size("event")
    ns = lax.axis_size("slab")
    nb = ne * ns
    blk, rows_b, _ = model.shape
    planes, ny, nz = wave_now.shape[1:]
    steps = adjoint.shape[1]
    reach = (coeffs_x.shape[2] - 1) // 2
    tiles_y = block_index.shape[2]
    n_tiles = planes * tiles_y
    rows_t = ny // tiles_y
    ids = jnp.swapaxes(block_index, 1, 2)
    coeffs = jnp.transpose(coeffs_x, (2, 0, 1))
    cfg = (ne, ns, planes, reach, steps, n_tiles, rows_t, blk, rows_b)
    arrays = (
        wave_prev,
        wave_now,
        adjoint,
        background,
        coeffs,
        live_count,
        stiff_y,
        stiff_z,
        interp_y,
        interp_z,
        model,
        ids,
    )
    arrays = [
        a if a is live_count else pltpu.with_memory_space_constraint(a, pltpu.HBM) for a in arrays
    ]
    dma = pltpu.SemaphoreType.DMA
    vmem = pltpu.VMEM
    slot = (rows_b, nz)

    def buffers():
        return [
            vmem((ne, ns) + slot, BF16),
            vmem((ns, ne) + slot, BF16),
            vmem((ne, ns) + slot, BF16),
            vmem((ns, ne) + slot, BF16),
        ]

    def sems():
        return [dma((n,)) for n in (ne, ne, ns, ns, ns, ns, ne, ne)] + [dma((4,))]

    grads = buffers()
    whole = pl.BlockSpec(memory_space=pltpu.VMEM)
    smem = pl.BlockSpec(memory_space=pltpu.SMEM)
    hbm = pl.BlockSpec(memory_space=pltpu.HBM)
    free = pl.BlockSpec(memory_space=pl.ANY)
    wave, grad = pl.pallas_call(
        functools.partial(window_kernel, cfg),
        out_shape=(
            jax.ShapeDtypeStruct(wave_now.shape, F32),
            jax.ShapeDtypeStruct(model.shape, F32),
        ),
        in_specs=[hbm] * 5 + [smem] + [hbm] * 6,
        out_specs=(free, whole),
        scratch_shapes=[
            vmem((planes + 2 * reach, ny, nz), F32),
            vmem((planes + 2 * reach, ny, nz), F32),
            vmem((planes, 2, ny, nz), BF16),
            vmem((planes, ny, nz), F32),
            vmem((planes, ny, nz), F32),
            vmem((steps, planes, ny, nz), F32),
            vmem((planes, ny, nz), F32),
            vmem((steps, 2, reach, ny, nz), BF16),
            vmem((2 * ny, 2 * ny), BF16),
            vmem((2 * nz, 2 * nz), BF16),
            vmem((ny, 2 * tiles_y * rows_b), BF16),
            vmem((tiles_y * rows_b, ny), BF16),
            vmem((2 * nz, nz), BF16),
            pltpu.SMEM(coeffs.shape, F32),
            vmem(stiff_y.shape, F32),
            vmem(stiff_z.shape, F32),
            vmem(interp_y.shape, BF16),
            vmem(interp_z.shape, BF16),
            vmem(ids.shape, I32),
            vmem((ROWS, LANES), I32),
            vmem((LANES // ROWS, ROWS, LANES), I32),
            vmem((ROWS, LANES), I32),
            vmem((ROWS, LANES), I32),
            vmem((ne, ROWS, LANES), I32),
            pltpu.SMEM((ROWS, LANES), I32),
            pltpu.SMEM((ROWS, LANES), I32),
            vmem((ne,) + model.shape, BF16),
            vmem((ns, 2 * ne) + slot, BF16),
            vmem((2 * nb + 1,) + slot, BF16),
            vmem((n_tiles + 1,) + slot, BF16),
            *grads,
            vmem((2, ne, ns) + slot, BF16),
            vmem((blk * rows_b, 2 * nb * rows_b), BF16),
            dma((3 + steps,)),
            dma((6,)),
            dma((3,)),
            dma((ns,)),
            dma((ns,)),
            dma((ne,)),
            dma((ne,)),
            dma((ne // 2,)),
            dma((ne // 2,)),
            dma((ne,)),
            dma((ne,)),
            dma((ns,)),
            dma((ns,)),
            dma((steps, 2)),
            dma((steps, 2)),
            dma,
            *sems(),
            dma,
        ],
        compiler_params=pltpu.CompilerParams(
            collective_id=0, has_side_effects=True, vmem_limit_bytes=40 * 1024 * 1024
        ),
        name="window",
    )(*arrays)
    return wave, grad


def solution(mesh):
    return jax.shard_map(
        shards,
        mesh=mesh,
        in_specs=(
            P("event", "slab", None, None),
            P("event", "slab", None, None),
            P("event", None, "slab", None, None),
            P("event", "slab", None, None),
            P("event", "slab", None),
            P(),
            P(),
            P(),
            P(),
            P(("event", "slab"), None, None),
            P("event", "slab", None),
            P("event", "slab"),
        ),
        out_specs=(P("event", "slab", None, None), P(("event", "slab"), None, None)),
        check_vma=False,
    )
```

```python
import functools
import math

import jax
import jax.numpy as jnp
from jax import lax
from jax.experimental import pallas as pl
from jax.experimental.pallas import tpu as pltpu
from jax.sharding import PartitionSpec as P

F32 = jnp.float32
BF16 = jnp.bfloat16
I32 = jnp.int32
MESH = pl.DeviceIdType.MESH
ROWS = 8
LANES = 128


def split(value):
    high = value.astype(BF16)
    low = (value - high.astype(F32)).astype(BF16)
    return high, low


def iota(shape, dim):
    return lax.broadcasted_iota(I32, shape, dim)


def dot(a, b):
    return jnp.dot(a, b, preferred_element_type=F32)


def window_kernel(
    cfg,
    prev_hbm,
    now_hbm,
    adj_hbm,
    back_hbm,
    coeffs_hbm,
    live,
    stiff_y_hbm,
    stiff_z_hbm,
    interp_y_hbm,
    interp_z_hbm,
    model,
    ids_hbm,
    wave_out,
    grad_out,
    u_a,
    u_b,
    u_hl,
    speed,
    kern,
    adj,
    ku0,
    halo,
    w_y,
    w_z,
    w_fwd,
    w_bwd,
    w_iz,
    coeffs,
    stiff_y,
    stiff_z,
    interp_y,
    interp_z,
    ids_in,
    id_own,
    id_all,
    idx_own,
    idx_req,
    asked_all,
    own_sm,
    req_sm,
    column,
    f_out,
    f_in,
    g_tiles,
    g_a,
    g_b,
    g_ra,
    g_rb,
    g_in,
    one_hot,
    load_sem,
    small_sem,
    idx_sem,
    id_send,
    id_recv,
    col_send,
    col_recv,
    pair_send,
    pair_recv,
    ask_send,
    ask_recv,
    f_send,
    f_recv,
    h_send,
    h_recv,
    f_loc,
    ga1_send,
    ga1_recv,
    ga2_send,
    ga2_recv,
    gb1_send,
    gb1_recv,
    gb2_send,
    gb2_recv,
    g_loc,
    out_sem,
):
    ne, ns, planes, reach, steps, n_tiles, rows_t, blk, rows_b = cfg
    nb = ne * ns
    e = lax.axis_index("event")
    s = lax.axis_index("slab")
    tiles_y = LANES // rows_t

    load_now = pltpu.make_async_copy(now_hbm.at[0], u_a.at[pl.ds(reach, planes)], load_sem.at[0])
    load_prev = pltpu.make_async_copy(prev_hbm.at[0], u_b.at[pl.ds(reach, planes)], load_sem.at[1])
    load_back = pltpu.make_async_copy(back_hbm.at[0], speed, load_sem.at[2])
    load_adj = [
        pltpu.make_async_copy(adj_hbm.at[0, i], adj.at[i], load_sem.at[3 + i]) for i in range(steps)
    ]
    load_coeffs = pltpu.make_async_copy(coeffs_hbm, coeffs, idx_sem.at[2])
    load_ids = pltpu.make_async_copy(ids_hbm, ids_in, small_sem.at[0])
    load_model = pltpu.make_async_copy(model, column.at[e], small_sem.at[1])
    load_weights = [
        pltpu.make_async_copy(stiff_y_hbm, stiff_y, small_sem.at[2]),
        pltpu.make_async_copy(stiff_z_hbm, stiff_z, small_sem.at[3]),
        pltpu.make_async_copy(interp_y_hbm, interp_y, small_sem.at[4]),
        pltpu.make_async_copy(interp_z_hbm, interp_z, small_sem.at[5]),
    ]
    load_ids.start()
    load_model.start()

    nz = ne // 2
    side_len = math.isqrt(ns)
    z, core = e // 2, lax.rem(e, 2)
    row, col = s // side_len, lax.rem(s, side_len)

    def event_at(d):
        return lax.rem(z + d // 2, nz) * 2 + lax.rem(core + d % 2, 2)

    def slab_at(d):
        y = lax.rem(row + d // side_len, side_len)
        return y * side_len + lax.rem(col + d % side_len, side_len)

    def around(d, n):
        return min(d, n - d)

    event_order = sorted(range(1, ne), key=lambda d: -around(d // 2, nz))
    slab_order = sorted(
        range(1, ns),
        key=lambda d: -around(d // side_len, side_len) - around(d % side_len, side_len),
    )

    barrier = pltpu.get_barrier_semaphore()
    for d in slab_order:
        pl.semaphore_signal(barrier, inc=1, device_id=(e, slab_at(d)), device_id_type=MESH)
    for d in event_order:
        pl.semaphore_signal(barrier, inc=1, device_id=(event_at(d), s), device_id_type=MESH)
    load_now.start()
    for c in load_weights:
        c.start()
    load_coeffs.start()
    load_back.start()
    load_prev.start()

    def event_copy(src, dst, send, recv, d, at=None):
        at = d if at is None else at
        return pltpu.make_async_remote_copy(
            src_ref=src,
            dst_ref=dst,
            send_sem=send.at[at],
            recv_sem=recv.at[at],
            device_id=(event_at(d), s),
            device_id_type=MESH,
        )

    def slab_copy(src, dst, send, recv, d, at=None):
        at = d if at is None else at
        return pltpu.make_async_remote_copy(
            src_ref=src,
            dst_ref=dst,
            send_sem=send.at[at],
            recv_sem=recv.at[at],
            device_id=(e, slab_at(d)),
            device_id_type=MESH,
        )

    far = [
        event_copy(column.at[e], column.at[e], col_send, col_recv, 2 * d) for d in range(1, nz)
    ]
    mine = [event_at(2 * ((nz - d) % nz)) for d in range(nz)]
    near = [
        event_copy(column.at[mine[d]], column.at[mine[d]], pair_send, pair_recv, 1, d)
        for d in range(nz)
    ]
    load_ids.wait()
    sub = iota((ROWS, LANES), 0)
    planes_id = ids_in[0]
    ids_row = jnp.concatenate([planes_id[q : q + 1] for q in range(tiles_y)], axis=1)
    if n_tiles < LANES:
        ids_row = jnp.concatenate([ids_row, jnp.full((1, LANES - n_tiles), -1, I32)], axis=1)
    ids = jnp.broadcast_to(ids_row, (ROWS, LANES))
    id_own[...] = ids
    for i in range(LANES // ROWS):
        if i >= ns:
            id_all[i] = jnp.full((ROWS, LANES), -1, I32)
    id_all[s] = ids
    pl.semaphore_wait(barrier, ne - 1 + ns - 1)
    id_copies = [slab_copy(id_own, id_all.at[s], id_send, id_recv, d) for d in slab_order]
    for c in id_copies:
        c.start()
    load_model.wait()
    for c in far[::-1]:
        c.start()
    near[0].start()
    for c in load_adj:
        c.start()

    owners = lax.shift_right_arithmetic(jnp.broadcast_to(ids_row, (LANES, LANES)), cfg_shift(blk))
    owners_t = jnp.transpose(owners)
    row_i = iota((LANES, LANES), 0)
    lane_i = iota((LANES, LANES), 1)
    earlier = jnp.where((owners == owners_t) & (row_i < lane_i), 1, 0)
    rank = jnp.sum(earlier, axis=0, keepdims=True)
    owner_row = owners[0:1]
    at_e = owner_row // ns
    at_s = owner_row - at_e * ns
    live_n = live[0, 0]

    def in_order(lane):
        return lane % planes * tiles_y + lane // planes

    address = at_s * (2 * ne) + rank * ne + at_e
    alive = in_order(iota((1, LANES), 1)) < live_n
    address = jnp.where(alive, address, 2 * nb)
    none = LANES
    match = owners == row_i
    first = jnp.min(jnp.where(match, lane_i, none), axis=1, keepdims=True)
    second = jnp.min(jnp.where(match & (lane_i > first), lane_i, none), axis=1, keepdims=True)

    def as_row(values):
        return jnp.transpose(jnp.broadcast_to(values, (LANES, LANES)))[0:1]

    def tile_at(lane):
        tile = in_order(lane)
        return jnp.where((lane < none) & (tile < live_n), tile, n_tiles)

    tile_0 = tile_at(as_row(first))
    tile_1 = tile_at(as_row(second))
    idx_own[...] = jnp.where(
        sub == 0,
        jnp.broadcast_to(address, (ROWS, LANES)),
        jnp.where(
            sub == 1,
            jnp.broadcast_to(tile_0, (ROWS, LANES)),
            jnp.broadcast_to(tile_1, (ROWS, LANES)),
        ),
    )
    own_copy = pltpu.make_async_copy(idx_own, own_sm, idx_sem.at[0])
    own_copy.start()

    for c in load_weights:
        c.wait()
    high, low = split(stiff_y[...])
    w_y[...] = jnp.concatenate(
        [jnp.concatenate([high, high], axis=1), jnp.concatenate([low, low], axis=1)], axis=0
    )
    high, low = split(jnp.transpose(stiff_z[...]))
    half = jnp.concatenate([high, low], axis=1)
    w_z[...] = jnp.concatenate([half, half], axis=0)

    load_now.wait()

    def split_planes(i, carry):
        high, low = split(u_a[reach + i])
        u_hl[i, 0] = high
        u_hl[i, 1] = low
        return carry

    def halo_copy(step, side):
        start = 0 if side == 0 else planes - reach
        return pltpu.make_async_remote_copy(
            src_ref=u_hl.at[pl.ds(start, reach), 0],
            dst_ref=halo.at[step, side],
            send_sem=h_send.at[step, side],
            recv_sem=h_recv.at[step, side],
            device_id=(e, lax.rem(s + (ns - 1 if side == 0 else 1), ns)),
            device_id_type=MESH,
        )

    def send_halo(step, side):
        @pl.when(s > 0 if side == 0 else s < ns - 1)
        def _():
            halo_copy(step, side).start()

    def take_halo(step, side):
        @pl.when(s > 0 if side == 0 else s < ns - 1)
        def _():
            halo_copy(step, side).wait_send()
            halo_copy(step, 1 - side).wait_recv()

    lax.fori_loop(0, reach, split_planes, 0, unroll=2)
    lax.fori_loop(planes - reach, planes, split_planes, 0, unroll=2)
    send_halo(0, 0)
    send_halo(0, 1)
    for d in range(1, nz):
        far[d - 1].wait_recv()
        near[d].start()
    lax.fori_loop(reach, planes - reach, split_planes, 0, unroll=2)
    for side in range(2):

        @pl.when(s == (0 if side == 0 else ns - 1))
        def _():
            halo[:, 1 - side] = jnp.zeros((steps, reach) + u_a.shape[1:], BF16)

    for c in id_copies:
        c.wait_recv()
    asked_ids = id_all[...].reshape(LANES, LANES)
    wanted = (row_i % ROWS) * ns + s
    asks = (lax.shift_right_arithmetic(asked_ids, cfg_shift(blk)) == wanted) & (row_i % ROWS < ne)
    code = lane_i * blk + (asked_ids & (blk - 1))
    none = LANES * blk
    code_0 = jnp.min(jnp.where(asks, code, none), axis=1, keepdims=True)
    code_1 = jnp.min(jnp.where(asks & (code > code_0), code, none), axis=1, keepdims=True)
    asked_0 = as_row(code_0) & (blk - 1)
    asked_1 = as_row(code_1) & (blk - 1)
    asked = jnp.where(
        sub == 0,
        jnp.broadcast_to(asked_0, (ROWS, LANES)),
        jnp.broadcast_to(asked_1, (ROWS, LANES)),
    )
    idx_req[...] = asked
    req_copy = pltpu.make_async_copy(idx_req, req_sm, idx_sem.at[1])
    req_copy.start()
    asked_all[e] = asked
    for c in near:
        c.wait_recv()
    req_copy.wait()
    fetches = []
    for d in slab_order + [0]:
        to = slab_at(d)
        for j in range(ne):
            f_out[to, j] = column[j, req_sm[0, to * ROWS + j]]
            f_out[to, ne + j] = column[j, req_sm[1, to * ROWS + j]]
        dst = f_in.at[pl.ds(s * (2 * ne), 2 * ne)]
        if d == 0:
            c = pltpu.make_async_copy(f_out.at[to], dst, f_loc)
        else:
            c = slab_copy(f_out.at[to], dst, f_send, f_recv, d)
        c.start()
        fetches.append(c)
    ask_copies = [
        event_copy(idx_req, asked_all.at[e], ask_send, ask_recv, d) for d in event_order
    ]
    for c in ask_copies:
        c.start()
    for c in id_copies + far + near:
        c.wait_send()

    half_rows = tiles_y * rows_b
    pick_b = jnp.where(iota((half_rows, rows_b), 0) % rows_b == iota((half_rows, rows_b), 1), 1.0, 0.0)
    pick_y = jnp.where(iota((rows_t, LANES), 1) % rows_t == iota((rows_t, LANES), 0), 1.0, 0.0)
    wide = dot(pick_b.astype(BF16), interp_y[...]).astype(BF16)
    wide = dot(wide, pick_y.astype(BF16))
    on_diag = iota((half_rows, LANES), 0) // rows_b == iota((half_rows, LANES), 1) // rows_t
    diag = jnp.where(on_diag, wide, 0.0)
    w_bwd[...] = diag.astype(BF16)
    w_fwd[...] = jnp.transpose(jnp.concatenate([diag, diag], axis=0)).astype(BF16)
    iz_t = jnp.transpose(interp_z[...].astype(F32)).astype(BF16)
    w_iz[...] = jnp.concatenate([iz_t, iz_t], axis=0)

    ny = LANES

    def stiff_pair(x):
        a, b = u_hl[x, 0], u_hl[x, 1]
        c, d = u_hl[x + 1, 0], u_hl[x + 1, 1]
        left = jnp.concatenate(
            [jnp.concatenate([a, b], axis=1), jnp.concatenate([c, d], axis=1)], axis=0
        )
        right = jnp.concatenate(
            [jnp.concatenate([a, c], axis=1), jnp.concatenate([b, d], axis=1)], axis=0
        )
        along_z = dot(left, w_z[...])
        along_z = along_z[:, :LANES] + along_z[:, LANES:]
        along_y = dot(w_y[...], right)
        along_y = along_y[:ny] + along_y[ny:]
        return along_z[:ny] + along_y[:, :LANES], along_z[ny:] + along_y[:, LANES:]

    def stencil(buf, x):
        total = coeffs[0, 0, x] * buf[x]
        for k in range(1, 2 * reach + 1):
            total = total + coeffs[k, 0, x] * buf[x + k]
        return total

    pairs = planes // 2
    edge = reach // 2

    def over_interior(body, unroll=6):
        def interior(i, carry):
            body(2 * i)
            return carry

        lax.fori_loop(edge, pairs - edge, interior, 0, unroll=unroll)

    def side_planes(side):
        return range(reach) if side == 0 else range(planes - reach, planes)

    def over_edge(body, side):
        start = 0 if side == 0 else pairs - edge

        def one(i, carry):
            body(2 * i)
            return carry

        lax.fori_loop(start, start + edge, one, 0, unroll=2)

    def own_part(buf, side):
        for x in side_planes(side)[::2]:
            for p, part in enumerate(stiff_pair(x)):
                total = part
                for k in range(2 * reach + 1):
                    if 0 <= x + p + k - reach < planes:
                        total = total + coeffs[k, 0, x + p] * buf[x + p + k]
                ku0[x + p] = total

    def whole_part(step, x):
        total = ku0[x]
        for k in range(2 * reach + 1):
            at = x + k - reach
            if at < 0:
                total = total + coeffs[k, 0, x] * halo[step, 1, at + reach].astype(F32)
            if at >= planes:
                total = total + coeffs[k, 0, x] * halo[step, 0, at - planes].astype(F32)
        return total

    def first_stiff(x):
        for p, part in enumerate(stiff_pair(x)):
            ku0[x + p] = part + stencil(u_a, x + p)

    load_coeffs.wait()
    over_interior(first_stiff)
    for side in range(2):
        own_part(u_a, side)
    for side in range(2):
        take_halo(0, side)
        for x in side_planes(side):
            ku0[x] = whole_part(0, x)
    f_in[2 * nb] = jnp.zeros(f_in.shape[1:], BF16)
    own_copy.wait()
    load_back.wait()
    load_prev.wait()
    for c in fetches[:-1]:
        c.wait_recv()
    for c in fetches[:-1]:
        c.wait_send()
    fetches[-1].wait()

    def speed_pair(x):
        blocks = jnp.concatenate(
            [f_in[own_sm[0, q * planes + x + p]] for p in range(2) for q in range(tiles_y)], axis=0
        )
        high, low = split(dot(blocks, interp_z[...]))
        right = jnp.concatenate(
            [
                jnp.concatenate([high[:half_rows], high[half_rows:]], axis=1),
                jnp.concatenate([low[:half_rows], low[half_rows:]], axis=1),
            ],
            axis=0,
        )
        perturb = dot(w_fwd[...], right)
        for p in range(2):
            speed[x + p] = speed[x + p] * jnp.exp(perturb[:, p * LANES : (p + 1) * LANES])

    def grad_pair(x):
        right = jnp.concatenate([u_hl[x, 1], u_hl[x + 1, 1]], axis=1)
        back = dot(w_bwd[...], right)
        parts = []
        for p in range(2):
            high, low = split(back[:, p * LANES : (p + 1) * LANES])
            parts.append(jnp.concatenate([high, low], axis=1))
        grads = dot(jnp.concatenate(parts, axis=0), w_iz[...])
        g_tiles[pl.ds(x * tiles_y, 2 * tiles_y)] = grads.astype(BF16).reshape(
            2 * tiles_y, rows_b, LANES
        )

    g_tiles[n_tiles] = jnp.zeros(g_tiles.shape[1:], BF16)

    def advance(x, force, step, now, prev):
        change = speed[x] * force
        drawn = adj[step, x] * change
        if step == steps - 1:
            ku0[x] = change
            u_hl[x, 1] = (kern[x] - drawn).astype(BF16)
            return
        if step == 0:
            kern[x] = -drawn
        else:
            kern[x] = kern[x] - drawn
        later = 2.0 * now[x + reach] - prev[x + reach] - change
        prev[x + reach] = later
        high, low = split(later)
        u_hl[x, 0] = high
        u_hl[x, 1] = low

    load_adj[0].wait()

    def first_step(x):
        speed_pair(x)
        for p in range(2):
            advance(x + p, ku0[x + p], 0, u_a, u_b)

    for side in range(2):
        over_edge(first_step, side)
        send_halo(1, side)
    over_interior(first_step)
    now, prev = u_b, u_a
    for step in range(1, steps):
        load_adj[step].wait()

        def body(x):
            parts = stiff_pair(x)
            for p in range(2):
                advance(x + p, parts[p] + stencil(now, x + p), step, now, prev)

        over_interior(body)
        for side in range(2):
            own_part(now, side)
        last = step == steps - 1
        if last:
            over_interior(grad_pair, 4)
        for i in range(2):
            side = (step + i) % 2
            take_halo(step, side)
            for x in side_planes(side):
                advance(x, whole_part(step, x), step, now, prev)
            if last:
                over_edge(grad_pair, side)
            else:
                send_halo(step + 1, side)
        now, prev = prev, now
    now, prev = prev, now

    events, slabs = event_order + [0], slab_order + [0]
    chunks = 2
    many_e, many_s = ne // chunks, ns // chunks

    def pack_event(d, h):
        to = event_at(d)
        part = pl.ds(h * many_s, many_s)
        for i in range(h * many_s, (h + 1) * many_s):
            g_a[to, i] = g_tiles[own_sm[1, to * ns + slab_at(slabs[i])]]
        src, dst = g_a.at[to, part], g_ra.at[e, part]
        if d == 0:
            return pltpu.make_async_copy(src, dst, g_loc.at[h])
        return event_copy(src, dst, ga1_send, ga1_recv, d, h * ne + d)

    def pack_slab(d, h):
        to = slab_at(d)
        part = pl.ds(h * many_e, many_e)
        for i in range(h * many_e, (h + 1) * many_e):
            g_b[to, i] = g_tiles[own_sm[2, event_at(events[i]) * ns + to]]
        src, dst = g_b.at[to, part], g_rb.at[s, part]
        if d == 0:
            return pltpu.make_async_copy(src, dst, g_loc.at[2 + h])
        return slab_copy(src, dst, gb1_send, gb1_recv, d, h * ns + d)

    a1, b1 = [], []
    for h in range(chunks):
        a1.append([])
        b1.append([])
        for i in range(max(ne, ns // 2)):
            for d in events[i : i + 1]:
                a1[h].append(pack_event(d, h))
                a1[h][-1].start()
            for d in slabs[2 * i : 2 * i + 2]:
                b1[h].append(pack_slab(d, h))
                b1[h][-1].start()
    a2, b2 = [], []
    for i, d in enumerate(slabs):
        if d == 0:
            a2.append(pltpu.make_async_copy(g_ra.at[:, i], g_in.at[0, :, s], g_loc.at[4]))
        else:
            a2.append(slab_copy(g_ra.at[:, i], g_in.at[0, :, s], ga2_send, ga2_recv, d))
    for i, d in enumerate(events):
        if d == 0:
            b2.append(pltpu.make_async_copy(g_rb.at[:, i], g_in.at[1, e], g_loc.at[5]))
        else:
            b2.append(event_copy(g_rb.at[:, i], g_in.at[1, e], gb2_send, gb2_recv, d))

    def arrive(copies):
        for c in copies[:-1]:
            c.wait_recv()
        copies[-1].wait()

    def last_wave(i, carry):
        prev[reach + i] = 2.0 * now[reach + i] - prev[reach + i] - ku0[i]
        return carry

    lax.fori_loop(0, planes, last_wave, 0)
    wave_copy = pltpu.make_async_copy(prev.at[pl.ds(reach, planes)], wave_out.at[0], out_sem)
    wave_copy.start()
    for h in range(chunks):
        arrive(a1[h])
        for c in a2[h * many_s : (h + 1) * many_s]:
            c.start()
        arrive(b1[h])
        for c in b2[h * many_e : (h + 1) * many_e]:
            c.start()

    for c in ask_copies:
        c.wait_recv()
    ranks = []
    for r in range(2):
        table = jnp.zeros((ROWS, LANES), I32)
        for i in range(ne):
            table = jnp.where(
                sub == i, jnp.broadcast_to(asked_all[i][r : r + 1], (ROWS, LANES)), table
            )
        ranks.append(table)
    width = ns * rows_b
    lane = iota((LANES, width), 1)
    pick = jnp.where(iota((LANES, width), 0) == lane // rows_b * ROWS + e, 1.0, 0.0)
    asked_both = jnp.concatenate(ranks, axis=0).astype(F32).astype(BF16)
    keys = dot(asked_both, pick.astype(BF16)).astype(I32) * rows_b
    keys = keys + iota((2 * ROWS, width), 1) % rows_b
    rows = iota((blk * rows_b, width), 0)
    for r in range(2):
        for i in range(ne):
            key = keys[r * ROWS + i : r * ROWS + i + 1]
            hot = jnp.where(jnp.broadcast_to(key, rows.shape) == rows, 1.0, 0.0)
            at = (r * ne + i) * width
            one_hot[:, at : at + width] = hot.astype(BF16)
    half_slots = nb * rows_b
    arrive(a2)
    total = dot(one_hot[:, :half_slots], g_in[0].reshape(half_slots, LANES))
    arrive(b2)
    total = total + dot(one_hot[:, half_slots:], g_in[1].reshape(half_slots, LANES))
    grad_out[...] = total.reshape(grad_out.shape)
    for h in range(chunks):
        for c in a1[h][:-1] + b1[h][:-1]:
            c.wait_send()
    for c in a2[:-1] + b2[:-1] + ask_copies:
        c.wait_send()
    wave_copy.wait()


def cfg_shift(blk):
    return blk.bit_length() - 1


def shards(
    wave_prev,
    wave_now,
    adjoint,
    background,
    coeffs_x,
    stiff_y,
    stiff_z,
    interp_y,
    interp_z,
    model,
    block_index,
    live_count,
):
    ne = lax.axis_size("event")
    ns = lax.axis_size("slab")
    nb = ne * ns
    blk, rows_b, _ = model.shape
    planes, ny, nz = wave_now.shape[1:]
    steps = adjoint.shape[1]
    reach = (coeffs_x.shape[2] - 1) // 2
    tiles_y = block_index.shape[2]
    n_tiles = planes * tiles_y
    rows_t = ny // tiles_y
    ids = jnp.swapaxes(block_index, 1, 2)
    coeffs = jnp.transpose(coeffs_x, (2, 0, 1))
    cfg = (ne, ns, planes, reach, steps, n_tiles, rows_t, blk, rows_b)
    arrays = (
        wave_prev,
        wave_now,
        adjoint,
        background,
        coeffs,
        live_count,
        stiff_y,
        stiff_z,
        interp_y,
        interp_z,
        model,
        ids,
    )
    arrays = [
        a if a is live_count else pltpu.with_memory_space_constraint(a, pltpu.HBM) for a in arrays
    ]
    dma = pltpu.SemaphoreType.DMA
    vmem = pltpu.VMEM
    slot = (rows_b, nz)

    def buffers():
        return [
            vmem((ne, ns) + slot, BF16),
            vmem((ns, ne) + slot, BF16),
            vmem((ne, ns) + slot, BF16),
            vmem((ns, ne) + slot, BF16),
        ]

    def sems():
        return [dma((n,)) for n in (2 * ne, 2 * ne, ns, ns, 2 * ns, 2 * ns, ne, ne)] + [dma((6,))]

    grads = buffers()
    whole = pl.BlockSpec(memory_space=pltpu.VMEM)
    smem = pl.BlockSpec(memory_space=pltpu.SMEM)
    hbm = pl.BlockSpec(memory_space=pltpu.HBM)
    free = pl.BlockSpec(memory_space=pl.ANY)
    wave, grad = pl.pallas_call(
        functools.partial(window_kernel, cfg),
        out_shape=(
            jax.ShapeDtypeStruct(wave_now.shape, F32),
            jax.ShapeDtypeStruct(model.shape, F32),
        ),
        in_specs=[hbm] * 5 + [smem] + [hbm] * 6,
        out_specs=(free, whole),
        scratch_shapes=[
            vmem((planes + 2 * reach, ny, nz), F32),
            vmem((planes + 2 * reach, ny, nz), F32),
            vmem((planes, 2, ny, nz), BF16),
            vmem((planes, ny, nz), F32),
            vmem((planes, ny, nz), F32),
            vmem((steps, planes, ny, nz), F32),
            vmem((planes, ny, nz), F32),
            vmem((steps, 2, reach, ny, nz), BF16),
            vmem((2 * ny, 2 * ny), BF16),
            vmem((2 * nz, 2 * nz), BF16),
            vmem((ny, 2 * tiles_y * rows_b), BF16),
            vmem((tiles_y * rows_b, ny), BF16),
            vmem((2 * nz, nz), BF16),
            pltpu.SMEM(coeffs.shape, F32),
            vmem(stiff_y.shape, F32),
            vmem(stiff_z.shape, F32),
            vmem(interp_y.shape, BF16),
            vmem(interp_z.shape, BF16),
            vmem(ids.shape, I32),
            vmem((ROWS, LANES), I32),
            vmem((LANES // ROWS, ROWS, LANES), I32),
            vmem((ROWS, LANES), I32),
            vmem((ROWS, LANES), I32),
            vmem((ne, ROWS, LANES), I32),
            pltpu.SMEM((ROWS, LANES), I32),
            pltpu.SMEM((ROWS, LANES), I32),
            vmem((ne,) + model.shape, BF16),
            vmem((ns, 2 * ne) + slot, BF16),
            vmem((2 * nb + 1,) + slot, BF16),
            vmem((n_tiles + 1,) + slot, BF16),
            *grads,
            vmem((2, ne, ns) + slot, BF16),
            vmem((blk * rows_b, 2 * nb * rows_b), BF16),
            dma((3 + steps,)),
            dma((6,)),
            dma((3,)),
            dma((ns,)),
            dma((ns,)),
            dma((ne,)),
            dma((ne,)),
            dma((ne // 2,)),
            dma((ne // 2,)),
            dma((ne,)),
            dma((ne,)),
            dma((ns,)),
            dma((ns,)),
            dma((steps, 2)),
            dma((steps, 2)),
            dma,
            *sems(),
            dma,
        ],
        compiler_params=pltpu.CompilerParams(
            collective_id=0, has_side_effects=True, vmem_limit_bytes=40 * 1024 * 1024
        ),
        name="window",
    )(*arrays)
    return wave, grad


def solution(mesh):
    return jax.shard_map(
        shards,
        mesh=mesh,
        in_specs=(
            P("event", "slab", None, None),
            P("event", "slab", None, None),
            P("event", None, "slab", None, None),
            P("event", "slab", None, None),
            P("event", "slab", None),
            P(),
            P(),
            P(),
            P(),
            P(("event", "slab"), None, None),
            P("event", "slab", None),
            P("event", "slab"),
        ),
        out_specs=(P("event", "slab", None, None), P(("event", "slab"), None, None)),
        check_vma=False,
    )
```

```python
import functools
import math

import jax
import jax.numpy as jnp
from jax import lax
from jax.experimental import pallas as pl
from jax.experimental.pallas import tpu as pltpu
from jax.sharding import PartitionSpec as P

F32 = jnp.float32
BF16 = jnp.bfloat16
I32 = jnp.int32
MESH = pl.DeviceIdType.MESH
ROWS = 8
LANES = 128


def split(value):
    high = value.astype(BF16)
    low = (value - high.astype(F32)).astype(BF16)
    return high, low


def iota(shape, dim):
    return lax.broadcasted_iota(I32, shape, dim)


def dot(a, b):
    return jnp.dot(a, b, preferred_element_type=F32)


def window_kernel(
    cfg,
    prev_hbm,
    now_hbm,
    adj_hbm,
    back_hbm,
    coeffs_hbm,
    live,
    stiff_y_hbm,
    stiff_z_hbm,
    interp_y_hbm,
    interp_z_hbm,
    model,
    ids_hbm,
    wave_out,
    grad_out,
    u_a,
    u_b,
    u_hl,
    speed,
    kern,
    adj,
    ku0,
    halo,
    w_y,
    w_z,
    w_fwd,
    w_bwd,
    w_iz,
    coeffs,
    stiff_y,
    stiff_z,
    interp_y,
    interp_z,
    ids_in,
    id_own,
    id_all,
    idx_own,
    idx_req,
    asked_all,
    own_sm,
    req_sm,
    column,
    f_out,
    f_in,
    g_tiles,
    g_a,
    g_b,
    g_ra,
    g_rb,
    g_in,
    one_hot,
    load_sem,
    small_sem,
    idx_sem,
    id_send,
    id_recv,
    col_send,
    col_recv,
    pair_send,
    pair_recv,
    ask_send,
    ask_recv,
    f_send,
    f_recv,
    h_send,
    h_recv,
    f_loc,
    ga1_send,
    ga1_recv,
    ga2_send,
    ga2_recv,
    gb1_send,
    gb1_recv,
    gb2_send,
    gb2_recv,
    g_loc,
    out_sem,
):
    ne, ns, planes, reach, steps, n_tiles, rows_t, blk, rows_b = cfg
    nb = ne * ns
    e = lax.axis_index("event")
    s = lax.axis_index("slab")
    tiles_y = LANES // rows_t

    load_now = pltpu.make_async_copy(now_hbm.at[0], u_a.at[pl.ds(reach, planes)], load_sem.at[0])
    load_prev = pltpu.make_async_copy(prev_hbm.at[0], u_b.at[pl.ds(reach, planes)], load_sem.at[1])
    load_back = pltpu.make_async_copy(back_hbm.at[0], speed, load_sem.at[2])
    load_adj = [
        pltpu.make_async_copy(adj_hbm.at[0, i], adj.at[i], load_sem.at[3 + i]) for i in range(steps)
    ]
    load_coeffs = pltpu.make_async_copy(coeffs_hbm, coeffs, idx_sem.at[2])
    load_ids = pltpu.make_async_copy(ids_hbm, ids_in, small_sem.at[0])
    load_model = pltpu.make_async_copy(model, column.at[e], small_sem.at[1])
    load_weights = [
        pltpu.make_async_copy(stiff_y_hbm, stiff_y, small_sem.at[2]),
        pltpu.make_async_copy(stiff_z_hbm, stiff_z, small_sem.at[3]),
        pltpu.make_async_copy(interp_y_hbm, interp_y, small_sem.at[4]),
        pltpu.make_async_copy(interp_z_hbm, interp_z, small_sem.at[5]),
    ]
    load_ids.start()
    load_model.start()

    nz = ne // 2
    side_len = math.isqrt(ns)
    z, core = e // 2, lax.rem(e, 2)
    row, col = s // side_len, lax.rem(s, side_len)

    def event_at(d):
        return lax.rem(z + d // 2, nz) * 2 + lax.rem(core + d % 2, 2)

    def slab_at(d):
        y = lax.rem(row + d // side_len, side_len)
        return y * side_len + lax.rem(col + d % side_len, side_len)

    def around(d, n):
        return min(d, n - d)

    event_order = sorted(range(1, ne), key=lambda d: -around(d // 2, nz))
    slab_order = sorted(
        range(1, ns),
        key=lambda d: -around(d // side_len, side_len) - around(d % side_len, side_len),
    )

    barrier = pltpu.get_barrier_semaphore()
    for d in slab_order:
        pl.semaphore_signal(barrier, inc=1, device_id=(e, slab_at(d)), device_id_type=MESH)
    for d in event_order:
        pl.semaphore_signal(barrier, inc=1, device_id=(event_at(d), s), device_id_type=MESH)
    load_now.start()
    for c in load_weights:
        c.start()
    load_coeffs.start()
    load_back.start()
    load_prev.start()

    def event_copy(src, dst, send, recv, d, at=None):
        at = d if at is None else at
        return pltpu.make_async_remote_copy(
            src_ref=src,
            dst_ref=dst,
            send_sem=send.at[at],
            recv_sem=recv.at[at],
            device_id=(event_at(d), s),
            device_id_type=MESH,
        )

    def slab_copy(src, dst, send, recv, d, at=None):
        at = d if at is None else at
        return pltpu.make_async_remote_copy(
            src_ref=src,
            dst_ref=dst,
            send_sem=send.at[at],
            recv_sem=recv.at[at],
            device_id=(e, slab_at(d)),
            device_id_type=MESH,
        )

    far_order = sorted(range(1, nz), key=lambda d: -around(d, nz))
    far = [
        event_copy(column.at[e], column.at[e], col_send, col_recv, 2 * d) for d in range(1, nz)
    ]
    mine = [event_at(2 * ((nz - d) % nz)) for d in range(nz)]
    near = [
        event_copy(column.at[mine[d]], column.at[mine[d]], pair_send, pair_recv, 1, d)
        for d in range(nz)
    ]
    load_ids.wait()
    sub = iota((ROWS, LANES), 0)
    planes_id = ids_in[0]
    ids_row = jnp.concatenate([planes_id[q : q + 1] for q in range(tiles_y)], axis=1)
    if n_tiles < LANES:
        ids_row = jnp.concatenate([ids_row, jnp.full((1, LANES - n_tiles), -1, I32)], axis=1)
    ids = jnp.broadcast_to(ids_row, (ROWS, LANES))
    id_own[...] = ids
    for i in range(LANES // ROWS):
        if i >= ns:
            id_all[i] = jnp.full((ROWS, LANES), -1, I32)
    id_all[s] = ids
    pl.semaphore_wait(barrier, ne - 1 + ns - 1)
    id_copies = [slab_copy(id_own, id_all.at[s], id_send, id_recv, d) for d in slab_order]
    load_model.wait()
    for d in far_order:
        far[d - 1].start()
    near[0].start()
    for c in id_copies:
        c.start()
    for c in load_adj:
        c.start()

    load_now.wait()

    def split_planes(i, carry):
        high, low = split(u_a[reach + i])
        u_hl[i, 0] = high
        u_hl[i, 1] = low
        return carry

    def halo_copy(step, side):
        start = 0 if side == 0 else planes - reach
        return pltpu.make_async_remote_copy(
            src_ref=u_hl.at[pl.ds(start, reach), 0],
            dst_ref=halo.at[step, side],
            send_sem=h_send.at[step, side],
            recv_sem=h_recv.at[step, side],
            device_id=(e, lax.rem(s + (ns - 1 if side == 0 else 1), ns)),
            device_id_type=MESH,
        )

    def send_halo(step, side):
        @pl.when(s > 0 if side == 0 else s < ns - 1)
        def _():
            halo_copy(step, side).start()

    def take_halo(step, side):
        @pl.when(s > 0 if side == 0 else s < ns - 1)
        def _():
            halo_copy(step, side).wait_send()
            halo_copy(step, 1 - side).wait_recv()

    lax.fori_loop(0, reach, split_planes, 0, unroll=2)
    lax.fori_loop(planes - reach, planes, split_planes, 0, unroll=2)
    send_halo(0, 0)
    send_halo(0, 1)
    for d in far_order[::-1]:
        far[d - 1].wait_recv()
        near[d].start()
    row_i = iota((LANES, LANES), 0)
    lane_i = iota((LANES, LANES), 1)

    def as_row(values):
        return jnp.transpose(jnp.broadcast_to(values, (LANES, LANES)))[0:1]

    for c in id_copies:
        c.wait_recv()
    asked_ids = id_all[...].reshape(LANES, LANES)
    wanted = (row_i % ROWS) * ns + s
    asks = (lax.shift_right_arithmetic(asked_ids, cfg_shift(blk)) == wanted) & (row_i % ROWS < ne)
    code = lane_i * blk + (asked_ids & (blk - 1))
    none = LANES * blk
    code_0 = jnp.min(jnp.where(asks, code, none), axis=1, keepdims=True)
    code_1 = jnp.min(jnp.where(asks & (code > code_0), code, none), axis=1, keepdims=True)
    asked_0 = as_row(code_0) & (blk - 1)
    asked_1 = as_row(code_1) & (blk - 1)
    asked = jnp.where(
        sub == 0,
        jnp.broadcast_to(asked_0, (ROWS, LANES)),
        jnp.broadcast_to(asked_1, (ROWS, LANES)),
    )
    idx_req[...] = asked
    req_copy = pltpu.make_async_copy(idx_req, req_sm, idx_sem.at[1])
    req_copy.start()
    asked_all[e] = asked
    for c in near:
        c.wait_recv()
    req_copy.wait()
    fetches = []
    for d in slab_order + [0]:
        to = slab_at(d)
        for j in range(ne):
            f_out[to, j] = column[j, req_sm[0, to * ROWS + j]]
            f_out[to, ne + j] = column[j, req_sm[1, to * ROWS + j]]
        dst = f_in.at[pl.ds(s * (2 * ne), 2 * ne)]
        if d == 0:
            c = pltpu.make_async_copy(f_out.at[to], dst, f_loc)
        else:
            c = slab_copy(f_out.at[to], dst, f_send, f_recv, d)
        c.start()
        fetches.append(c)
    ask_copies = [
        event_copy(idx_req, asked_all.at[e], ask_send, ask_recv, d) for d in event_order
    ]
    for c in ask_copies:
        c.start()
    for c in id_copies + far + near:
        c.wait_send()

    owners = lax.shift_right_arithmetic(jnp.broadcast_to(ids_row, (LANES, LANES)), cfg_shift(blk))
    owners_t = jnp.transpose(owners)
    earlier = jnp.where((owners == owners_t) & (row_i < lane_i), 1, 0)
    rank = jnp.sum(earlier, axis=0, keepdims=True)
    owner_row = owners[0:1]
    at_e = owner_row // ns
    at_s = owner_row - at_e * ns
    live_n = live[0, 0]

    def in_order(lane):
        return lane % planes * tiles_y + lane // planes

    address = at_s * (2 * ne) + rank * ne + at_e
    alive = in_order(iota((1, LANES), 1)) < live_n
    address = jnp.where(alive, address, 2 * nb)
    none = LANES
    match = owners == row_i
    first = jnp.min(jnp.where(match, lane_i, none), axis=1, keepdims=True)
    second = jnp.min(jnp.where(match & (lane_i > first), lane_i, none), axis=1, keepdims=True)

    def tile_at(lane):
        tile = in_order(lane)
        return jnp.where((lane < none) & (tile < live_n), tile, n_tiles)

    tile_0 = tile_at(as_row(first))
    tile_1 = tile_at(as_row(second))
    idx_own[...] = jnp.where(
        sub == 0,
        jnp.broadcast_to(address, (ROWS, LANES)),
        jnp.where(
            sub == 1,
            jnp.broadcast_to(tile_0, (ROWS, LANES)),
            jnp.broadcast_to(tile_1, (ROWS, LANES)),
        ),
    )
    own_copy = pltpu.make_async_copy(idx_own, own_sm, idx_sem.at[0])
    own_copy.start()

    for c in load_weights:
        c.wait()
    high, low = split(stiff_y[...])
    w_y[...] = jnp.concatenate(
        [jnp.concatenate([high, high], axis=1), jnp.concatenate([low, low], axis=1)], axis=0
    )
    high, low = split(jnp.transpose(stiff_z[...]))
    half = jnp.concatenate([high, low], axis=1)
    w_z[...] = jnp.concatenate([half, half], axis=0)

    lax.fori_loop(reach, planes - reach, split_planes, 0, unroll=2)
    for side in range(2):

        @pl.when(s == (0 if side == 0 else ns - 1))
        def _():
            halo[:, 1 - side] = jnp.zeros((steps, reach) + u_a.shape[1:], BF16)

    half_rows = tiles_y * rows_b
    pick_b = jnp.where(iota((half_rows, rows_b), 0) % rows_b == iota((half_rows, rows_b), 1), 1.0, 0.0)
    pick_y = jnp.where(iota((rows_t, LANES), 1) % rows_t == iota((rows_t, LANES), 0), 1.0, 0.0)
    wide = dot(pick_b.astype(BF16), interp_y[...]).astype(BF16)
    wide = dot(wide, pick_y.astype(BF16))
    on_diag = iota((half_rows, LANES), 0) // rows_b == iota((half_rows, LANES), 1) // rows_t
    diag = jnp.where(on_diag, wide, 0.0)
    w_bwd[...] = diag.astype(BF16)
    w_fwd[...] = jnp.transpose(jnp.concatenate([diag, diag], axis=0)).astype(BF16)
    iz_t = jnp.transpose(interp_z[...].astype(F32)).astype(BF16)
    w_iz[...] = jnp.concatenate([iz_t, iz_t], axis=0)

    ny = LANES

    def stiff_pair(x):
        a, b = u_hl[x, 0], u_hl[x, 1]
        c, d = u_hl[x + 1, 0], u_hl[x + 1, 1]
        left = jnp.concatenate(
            [jnp.concatenate([a, b], axis=1), jnp.concatenate([c, d], axis=1)], axis=0
        )
        right = jnp.concatenate(
            [jnp.concatenate([a, c], axis=1), jnp.concatenate([b, d], axis=1)], axis=0
        )
        along_z = dot(left, w_z[...])
        along_z = along_z[:, :LANES] + along_z[:, LANES:]
        along_y = dot(w_y[...], right)
        along_y = along_y[:ny] + along_y[ny:]
        return along_z[:ny] + along_y[:, :LANES], along_z[ny:] + along_y[:, LANES:]

    def stencil(buf, x):
        total = coeffs[0, 0, x] * buf[x]
        for k in range(1, 2 * reach + 1):
            total = total + coeffs[k, 0, x] * buf[x + k]
        return total

    pairs = planes // 2
    edge = reach // 2

    def over_interior(body, unroll=6):
        def interior(i, carry):
            body(2 * i)
            return carry

        lax.fori_loop(edge, pairs - edge, interior, 0, unroll=unroll)

    def side_planes(side):
        return range(reach) if side == 0 else range(planes - reach, planes)

    def over_edge(body, side):
        start = 0 if side == 0 else pairs - edge

        def one(i, carry):
            body(2 * i)
            return carry

        lax.fori_loop(start, start + edge, one, 0, unroll=2)

    def own_part(buf, side):
        for x in side_planes(side)[::2]:
            for p, part in enumerate(stiff_pair(x)):
                total = part
                for k in range(2 * reach + 1):
                    if 0 <= x + p + k - reach < planes:
                        total = total + coeffs[k, 0, x + p] * buf[x + p + k]
                ku0[x + p] = total

    def whole_part(step, x):
        total = ku0[x]
        for k in range(2 * reach + 1):
            at = x + k - reach
            if at < 0:
                total = total + coeffs[k, 0, x] * halo[step, 1, at + reach].astype(F32)
            if at >= planes:
                total = total + coeffs[k, 0, x] * halo[step, 0, at - planes].astype(F32)
        return total

    def first_stiff(x):
        for p, part in enumerate(stiff_pair(x)):
            ku0[x + p] = part + stencil(u_a, x + p)

    load_coeffs.wait()
    over_interior(first_stiff)
    for side in range(2):
        own_part(u_a, side)
    for side in range(2):
        take_halo(0, side)
        for x in side_planes(side):
            ku0[x] = whole_part(0, x)
    f_in[2 * nb] = jnp.zeros(f_in.shape[1:], BF16)
    own_copy.wait()
    load_back.wait()
    load_prev.wait()
    for c in fetches[:-1]:
        c.wait_recv()
    for c in fetches[:-1]:
        c.wait_send()
    fetches[-1].wait()

    def speed_pair(x):
        blocks = jnp.concatenate(
            [f_in[own_sm[0, q * planes + x + p]] for p in range(2) for q in range(tiles_y)], axis=0
        )
        high, low = split(dot(blocks, interp_z[...]))
        right = jnp.concatenate(
            [
                jnp.concatenate([high[:half_rows], high[half_rows:]], axis=1),
                jnp.concatenate([low[:half_rows], low[half_rows:]], axis=1),
            ],
            axis=0,
        )
        perturb = dot(w_fwd[...], right)
        for p in range(2):
            speed[x + p] = speed[x + p] * jnp.exp(perturb[:, p * LANES : (p + 1) * LANES])

    def grad_pair(x):
        right = jnp.concatenate([u_hl[x, 1], u_hl[x + 1, 1]], axis=1)
        back = dot(w_bwd[...], right)
        parts = []
        for p in range(2):
            high, low = split(back[:, p * LANES : (p + 1) * LANES])
            parts.append(jnp.concatenate([high, low], axis=1))
        grads = dot(jnp.concatenate(parts, axis=0), w_iz[...])
        g_tiles[pl.ds(x * tiles_y, 2 * tiles_y)] = grads.astype(BF16).reshape(
            2 * tiles_y, rows_b, LANES
        )

    g_tiles[n_tiles] = jnp.zeros(g_tiles.shape[1:], BF16)

    def advance(x, force, step, now, prev):
        change = speed[x] * force
        drawn = adj[step, x] * change
        if step == steps - 1:
            ku0[x] = change
            u_hl[x, 1] = (kern[x] - drawn).astype(BF16)
            return
        if step == 0:
            kern[x] = -drawn
        else:
            kern[x] = kern[x] - drawn
        later = 2.0 * now[x + reach] - prev[x + reach] - change
        prev[x + reach] = later
        high, low = split(later)
        u_hl[x, 0] = high
        u_hl[x, 1] = low

    load_adj[0].wait()

    def first_step(x):
        speed_pair(x)
        for p in range(2):
            advance(x + p, ku0[x + p], 0, u_a, u_b)

    for side in range(2):
        over_edge(first_step, side)
        send_halo(1, side)
    over_interior(first_step)
    now, prev = u_b, u_a
    for step in range(1, steps):
        load_adj[step].wait()

        def body(x):
            parts = stiff_pair(x)
            for p in range(2):
                advance(x + p, parts[p] + stencil(now, x + p), step, now, prev)

        over_interior(body)
        for side in range(2):
            own_part(now, side)
        last = step == steps - 1
        if last:
            over_interior(grad_pair, 4)
        for i in range(2):
            side = (step + i) % 2
            take_halo(step, side)
            for x in side_planes(side):
                advance(x, whole_part(step, x), step, now, prev)
            if last:
                over_edge(grad_pair, side)
            else:
                send_halo(step + 1, side)
        now, prev = prev, now
    now, prev = prev, now

    events, slabs = event_order + [0], slab_order + [0]
    chunks = 2
    many_e, many_s = ne // chunks, ns // chunks

    def pack_event(d, h):
        to = event_at(d)
        part = pl.ds(h * many_s, many_s)
        for i in range(h * many_s, (h + 1) * many_s):
            g_a[to, i] = g_tiles[own_sm[1, to * ns + slab_at(slabs[i])]]
        src, dst = g_a.at[to, part], g_ra.at[e, part]
        if d == 0:
            return pltpu.make_async_copy(src, dst, g_loc.at[h])
        return event_copy(src, dst, ga1_send, ga1_recv, d, h * ne + d)

    def pack_slab(d, h):
        to = slab_at(d)
        part = pl.ds(h * many_e, many_e)
        for i in range(h * many_e, (h + 1) * many_e):
            g_b[to, i] = g_tiles[own_sm[2, event_at(events[i]) * ns + to]]
        src, dst = g_b.at[to, part], g_rb.at[s, part]
        if d == 0:
            return pltpu.make_async_copy(src, dst, g_loc.at[2 + h])
        return slab_copy(src, dst, gb1_send, gb1_recv, d, h * ns + d)

    a1, b1 = [], []
    for h in range(chunks):
        a1.append([])
        b1.append([])
        for i in range(max(ne, ns // 2)):
            for d in events[i : i + 1]:
                a1[h].append(pack_event(d, h))
                a1[h][-1].start()
            for d in slabs[2 * i : 2 * i + 2]:
                b1[h].append(pack_slab(d, h))
                b1[h][-1].start()
    a2, b2 = [], []
    for i, d in enumerate(slabs):
        if d == 0:
            a2.append(pltpu.make_async_copy(g_ra.at[:, i], g_in.at[0, :, s], g_loc.at[4]))
        else:
            a2.append(slab_copy(g_ra.at[:, i], g_in.at[0, :, s], ga2_send, ga2_recv, d))
    for i, d in enumerate(events):
        if d == 0:
            b2.append(pltpu.make_async_copy(g_rb.at[:, i], g_in.at[1, e], g_loc.at[5]))
        else:
            b2.append(event_copy(g_rb.at[:, i], g_in.at[1, e], gb2_send, gb2_recv, d))

    def arrive(copies):
        for c in copies[:-1]:
            c.wait_recv()
        copies[-1].wait()

    def last_wave(i, carry):
        prev[reach + i] = 2.0 * now[reach + i] - prev[reach + i] - ku0[i]
        return carry

    lax.fori_loop(0, planes, last_wave, 0)
    wave_copy = pltpu.make_async_copy(prev.at[pl.ds(reach, planes)], wave_out.at[0], out_sem)
    wave_copy.start()
    for h in range(chunks):
        arrive(a1[h])
        for c in a2[h * many_s : (h + 1) * many_s]:
            c.start()
        arrive(b1[h])
        for c in b2[h * many_e : (h + 1) * many_e]:
            c.start()

    for c in ask_copies:
        c.wait_recv()
    ranks = []
    for r in range(2):
        table = jnp.zeros((ROWS, LANES), I32)
        for i in range(ne):
            table = jnp.where(
                sub == i, jnp.broadcast_to(asked_all[i][r : r + 1], (ROWS, LANES)), table
            )
        ranks.append(table)
    width = ns * rows_b
    lane = iota((LANES, width), 1)
    pick = jnp.where(iota((LANES, width), 0) == lane // rows_b * ROWS + e, 1.0, 0.0)
    asked_both = jnp.concatenate(ranks, axis=0).astype(F32).astype(BF16)
    keys = dot(asked_both, pick.astype(BF16)).astype(I32) * rows_b
    keys = keys + iota((2 * ROWS, width), 1) % rows_b
    rows = iota((blk * rows_b, width), 0)
    for r in range(2):
        for i in range(ne):
            key = keys[r * ROWS + i : r * ROWS + i + 1]
            hot = jnp.where(jnp.broadcast_to(key, rows.shape) == rows, 1.0, 0.0)
            at = (r * ne + i) * width
            one_hot[:, at : at + width] = hot.astype(BF16)
    half_slots = nb * rows_b
    arrive(a2)
    total = dot(one_hot[:, :half_slots], g_in[0].reshape(half_slots, LANES))
    arrive(b2)
    total = total + dot(one_hot[:, half_slots:], g_in[1].reshape(half_slots, LANES))
    grad_out[...] = total.reshape(grad_out.shape)
    for h in range(chunks):
        for c in a1[h][:-1] + b1[h][:-1]:
            c.wait_send()
    for c in a2[:-1] + b2[:-1] + ask_copies:
        c.wait_send()
    wave_copy.wait()


def cfg_shift(blk):
    return blk.bit_length() - 1


def shards(
    wave_prev,
    wave_now,
    adjoint,
    background,
    coeffs_x,
    stiff_y,
    stiff_z,
    interp_y,
    interp_z,
    model,
    block_index,
    live_count,
):
    ne = lax.axis_size("event")
    ns = lax.axis_size("slab")
    nb = ne * ns
    blk, rows_b, _ = model.shape
    planes, ny, nz = wave_now.shape[1:]
    steps = adjoint.shape[1]
    reach = (coeffs_x.shape[2] - 1) // 2
    tiles_y = block_index.shape[2]
    n_tiles = planes * tiles_y
    rows_t = ny // tiles_y
    ids = jnp.swapaxes(block_index, 1, 2)
    coeffs = jnp.transpose(coeffs_x, (2, 0, 1))
    cfg = (ne, ns, planes, reach, steps, n_tiles, rows_t, blk, rows_b)
    arrays = (
        wave_prev,
        wave_now,
        adjoint,
        background,
        coeffs,
        live_count,
        stiff_y,
        stiff_z,
        interp_y,
        interp_z,
        model,
        ids,
    )
    arrays = [
        a if a is live_count else pltpu.with_memory_space_constraint(a, pltpu.HBM) for a in arrays
    ]
    dma = pltpu.SemaphoreType.DMA
    vmem = pltpu.VMEM
    slot = (rows_b, nz)

    def buffers():
        return [
            vmem((ne, ns) + slot, BF16),
            vmem((ns, ne) + slot, BF16),
            vmem((ne, ns) + slot, BF16),
            vmem((ns, ne) + slot, BF16),
        ]

    def sems():
        return [dma((n,)) for n in (2 * ne, 2 * ne, ns, ns, 2 * ns, 2 * ns, ne, ne)] + [dma((6,))]

    grads = buffers()
    whole = pl.BlockSpec(memory_space=pltpu.VMEM)
    smem = pl.BlockSpec(memory_space=pltpu.SMEM)
    hbm = pl.BlockSpec(memory_space=pltpu.HBM)
    free = pl.BlockSpec(memory_space=pl.ANY)
    wave, grad = pl.pallas_call(
        functools.partial(window_kernel, cfg),
        out_shape=(
            jax.ShapeDtypeStruct(wave_now.shape, F32),
            jax.ShapeDtypeStruct(model.shape, F32),
        ),
        in_specs=[hbm] * 5 + [smem] + [hbm] * 6,
        out_specs=(free, whole),
        scratch_shapes=[
            vmem((planes + 2 * reach, ny, nz), F32),
            vmem((planes + 2 * reach, ny, nz), F32),
            vmem((planes, 2, ny, nz), BF16),
            vmem((planes, ny, nz), F32),
            vmem((planes, ny, nz), F32),
            vmem((steps, planes, ny, nz), F32),
            vmem((planes, ny, nz), F32),
            vmem((steps, 2, reach, ny, nz), BF16),
            vmem((2 * ny, 2 * ny), BF16),
            vmem((2 * nz, 2 * nz), BF16),
            vmem((ny, 2 * tiles_y * rows_b), BF16),
            vmem((tiles_y * rows_b, ny), BF16),
            vmem((2 * nz, nz), BF16),
            pltpu.SMEM(coeffs.shape, F32),
            vmem(stiff_y.shape, F32),
            vmem(stiff_z.shape, F32),
            vmem(interp_y.shape, BF16),
            vmem(interp_z.shape, BF16),
            vmem(ids.shape, I32),
            vmem((ROWS, LANES), I32),
            vmem((LANES // ROWS, ROWS, LANES), I32),
            vmem((ROWS, LANES), I32),
            vmem((ROWS, LANES), I32),
            vmem((ne, ROWS, LANES), I32),
            pltpu.SMEM((ROWS, LANES), I32),
            pltpu.SMEM((ROWS, LANES), I32),
            vmem((ne,) + model.shape, BF16),
            vmem((ns, 2 * ne) + slot, BF16),
            vmem((2 * nb + 1,) + slot, BF16),
            vmem((n_tiles + 1,) + slot, BF16),
            *grads,
            vmem((2, ne, ns) + slot, BF16),
            vmem((blk * rows_b, 2 * nb * rows_b), BF16),
            dma((3 + steps,)),
            dma((6,)),
            dma((3,)),
            dma((ns,)),
            dma((ns,)),
            dma((ne,)),
            dma((ne,)),
            dma((ne // 2,)),
            dma((ne // 2,)),
            dma((ne,)),
            dma((ne,)),
            dma((ns,)),
            dma((ns,)),
            dma((steps, 2)),
            dma((steps, 2)),
            dma,
            *sems(),
            dma,
        ],
        compiler_params=pltpu.CompilerParams(
            collective_id=0, has_side_effects=True, vmem_limit_bytes=40 * 1024 * 1024
        ),
        name="window",
    )(*arrays)
    return wave, grad


def solution(mesh):
    return jax.shard_map(
        shards,
        mesh=mesh,
        in_specs=(
            P("event", "slab", None, None),
            P("event", "slab", None, None),
            P("event", None, "slab", None, None),
            P("event", "slab", None, None),
            P("event", "slab", None),
            P(),
            P(),
            P(),
            P(),
            P(("event", "slab"), None, None),
            P("event", "slab", None),
            P("event", "slab"),
        ),
        out_specs=(P("event", "slab", None, None), P(("event", "slab"), None, None)),
        check_vma=False,
    )
```

```python
import functools
import math

import jax
import jax.numpy as jnp
from jax import lax
from jax.experimental import pallas as pl
from jax.experimental.pallas import tpu as pltpu
from jax.sharding import PartitionSpec as P

F32 = jnp.float32
BF16 = jnp.bfloat16
I32 = jnp.int32
MESH = pl.DeviceIdType.MESH
ROWS = 8
LANES = 128


def split(value):
    high = value.astype(BF16)
    low = (value - high.astype(F32)).astype(BF16)
    return high, low


def iota(shape, dim):
    return lax.broadcasted_iota(I32, shape, dim)


def dot(a, b):
    return jnp.dot(a, b, preferred_element_type=F32)


def window_kernel(
    cfg,
    prev_hbm,
    now_hbm,
    adj_hbm,
    back_hbm,
    coeffs_hbm,
    live,
    stiff_y_hbm,
    stiff_z_hbm,
    interp_y_hbm,
    interp_z_hbm,
    model,
    ids_hbm,
    wave_out,
    grad_out,
    u_a,
    u_b,
    u_hl,
    speed,
    kern,
    adj,
    ku0,
    halo,
    w_y,
    w_z,
    w_fwd,
    w_bwd,
    w_iz,
    coeffs,
    stiff_y,
    stiff_z,
    interp_y,
    interp_z,
    ids_in,
    id_own,
    id_all,
    idx_own,
    idx_req,
    asked_all,
    own_sm,
    req_sm,
    column,
    f_out,
    f_in,
    g_tiles,
    g_a,
    g_b,
    g_ra,
    g_rb,
    g_in,
    one_hot,
    load_sem,
    small_sem,
    idx_sem,
    id_send,
    id_recv,
    col_send,
    col_recv,
    pair_send,
    pair_recv,
    ask_send,
    ask_recv,
    f_send,
    f_recv,
    h_send,
    h_recv,
    f_loc,
    ga1_send,
    ga1_recv,
    ga2_send,
    ga2_recv,
    gb1_send,
    gb1_recv,
    gb2_send,
    gb2_recv,
    g_loc,
    out_sem,
):
    ne, ns, planes, reach, steps, n_tiles, rows_t, blk, rows_b = cfg
    nb = ne * ns
    e = lax.axis_index("event")
    s = lax.axis_index("slab")
    tiles_y = LANES // rows_t

    load_now = pltpu.make_async_copy(now_hbm.at[0], u_a.at[pl.ds(reach, planes)], load_sem.at[0])
    load_prev = pltpu.make_async_copy(prev_hbm.at[0], u_b.at[pl.ds(reach, planes)], load_sem.at[1])
    load_back = pltpu.make_async_copy(back_hbm.at[0], speed, load_sem.at[2])
    load_adj = [
        pltpu.make_async_copy(adj_hbm.at[0, i], adj.at[i], load_sem.at[3 + i]) for i in range(steps)
    ]
    load_coeffs = pltpu.make_async_copy(coeffs_hbm, coeffs, idx_sem.at[2])
    load_ids = pltpu.make_async_copy(ids_hbm, ids_in, small_sem.at[0])
    load_model = pltpu.make_async_copy(model, column.at[e], small_sem.at[1])
    load_weights = [
        pltpu.make_async_copy(stiff_y_hbm, stiff_y, small_sem.at[2]),
        pltpu.make_async_copy(stiff_z_hbm, stiff_z, small_sem.at[3]),
        pltpu.make_async_copy(interp_y_hbm, interp_y, small_sem.at[4]),
        pltpu.make_async_copy(interp_z_hbm, interp_z, small_sem.at[5]),
    ]
    load_ids.start()
    load_model.start()

    nz = ne // 2
    side_len = math.isqrt(ns)
    z, core = e // 2, lax.rem(e, 2)
    row, col = s // side_len, lax.rem(s, side_len)

    def event_at(d):
        return lax.rem(z + d // 2, nz) * 2 + lax.rem(core + d % 2, 2)

    def slab_at(d):
        y = lax.rem(row + d // side_len, side_len)
        return y * side_len + lax.rem(col + d % side_len, side_len)

    def around(d, n):
        return min(d, n - d)

    event_order = sorted(range(1, ne), key=lambda d: -around(d // 2, nz))
    slab_order = sorted(
        range(1, ns),
        key=lambda d: -around(d // side_len, side_len) - around(d % side_len, side_len),
    )

    barrier = pltpu.get_barrier_semaphore()
    for d in slab_order:
        pl.semaphore_signal(barrier, inc=1, device_id=(e, slab_at(d)), device_id_type=MESH)
    for d in event_order:
        pl.semaphore_signal(barrier, inc=1, device_id=(event_at(d), s), device_id_type=MESH)
    load_now.start()
    for c in load_weights:
        c.start()
    load_coeffs.start()
    load_back.start()
    load_prev.start()

    def event_copy(src, dst, send, recv, d, at=None):
        at = d if at is None else at
        return pltpu.make_async_remote_copy(
            src_ref=src,
            dst_ref=dst,
            send_sem=send.at[at],
            recv_sem=recv.at[at],
            device_id=(event_at(d), s),
            device_id_type=MESH,
        )

    def slab_copy(src, dst, send, recv, d, at=None):
        at = d if at is None else at
        return pltpu.make_async_remote_copy(
            src_ref=src,
            dst_ref=dst,
            send_sem=send.at[at],
            recv_sem=recv.at[at],
            device_id=(e, slab_at(d)),
            device_id_type=MESH,
        )

    far_order = sorted(range(1, nz), key=lambda d: -around(d, nz))
    far = [
        event_copy(column.at[e], column.at[e], col_send, col_recv, 2 * d) for d in range(1, nz)
    ]
    mine = [event_at(2 * ((nz - d) % nz)) for d in range(nz)]
    near = [
        event_copy(column.at[mine[d]], column.at[mine[d]], pair_send, pair_recv, 1, d)
        for d in range(nz)
    ]
    load_ids.wait()
    sub = iota((ROWS, LANES), 0)
    planes_id = ids_in[0]
    ids_row = jnp.concatenate([planes_id[q : q + 1] for q in range(tiles_y)], axis=1)
    if n_tiles < LANES:
        ids_row = jnp.concatenate([ids_row, jnp.full((1, LANES - n_tiles), -1, I32)], axis=1)
    ids = jnp.broadcast_to(ids_row, (ROWS, LANES))
    id_own[...] = ids
    for i in range(LANES // ROWS):
        if i >= ns:
            id_all[i] = jnp.full((ROWS, LANES), -1, I32)
    id_all[s] = ids
    pl.semaphore_wait(barrier, ne - 1 + ns - 1)
    id_copies = [slab_copy(id_own, id_all.at[s], id_send, id_recv, d) for d in slab_order]
    load_model.wait()
    for d in far_order:
        far[d - 1].start()
    near[0].start()
    for c in id_copies:
        c.start()
    for c in load_adj:
        c.start()

    load_now.wait()

    def split_planes(i, carry):
        high, low = split(u_a[reach + i])
        u_hl[i, 0] = high
        u_hl[i, 1] = low
        return carry

    def halo_copy(step, side):
        start = 0 if side == 0 else planes - reach
        return pltpu.make_async_remote_copy(
            src_ref=u_hl.at[pl.ds(start, reach), 0],
            dst_ref=halo.at[step, side],
            send_sem=h_send.at[step, side],
            recv_sem=h_recv.at[step, side],
            device_id=(e, lax.rem(s + (ns - 1 if side == 0 else 1), ns)),
            device_id_type=MESH,
        )

    def send_halo(step, side):
        @pl.when(s > 0 if side == 0 else s < ns - 1)
        def _():
            halo_copy(step, side).start()

    def take_halo(step, side):
        @pl.when(s > 0 if side == 0 else s < ns - 1)
        def _():
            halo_copy(step, side).wait_send()
            halo_copy(step, 1 - side).wait_recv()

    lax.fori_loop(0, reach, split_planes, 0, unroll=2)
    lax.fori_loop(planes - reach, planes, split_planes, 0, unroll=2)
    send_halo(0, 0)
    send_halo(0, 1)
    for d in far_order[::-1]:
        far[d - 1].wait_recv()
        near[d].start()
    row_i = iota((LANES, LANES), 0)
    lane_i = iota((LANES, LANES), 1)

    def as_row(values):
        return jnp.transpose(jnp.broadcast_to(values, (LANES, LANES)))[0:1]

    for c in id_copies:
        c.wait_recv()
    asked_ids = id_all[...].reshape(LANES, LANES)
    wanted = (row_i % ROWS) * ns + s
    asks = (lax.shift_right_arithmetic(asked_ids, cfg_shift(blk)) == wanted) & (row_i % ROWS < ne)
    code = lane_i * blk + (asked_ids & (blk - 1))
    none = LANES * blk
    code_0 = jnp.min(jnp.where(asks, code, none), axis=1, keepdims=True)
    code_1 = jnp.min(jnp.where(asks & (code > code_0), code, none), axis=1, keepdims=True)
    asked_0 = as_row(code_0) & (blk - 1)
    asked_1 = as_row(code_1) & (blk - 1)
    asked = jnp.where(
        sub == 0,
        jnp.broadcast_to(asked_0, (ROWS, LANES)),
        jnp.broadcast_to(asked_1, (ROWS, LANES)),
    )
    idx_req[...] = asked
    req_copy = pltpu.make_async_copy(idx_req, req_sm, idx_sem.at[1])
    req_copy.start()
    asked_all[e] = asked
    for c in near:
        c.wait_recv()
    req_copy.wait()
    fetches = []
    for d in slab_order + [0]:
        to = slab_at(d)
        for j in range(ne):
            f_out[to, j] = column[j, req_sm[0, to * ROWS + j]]
            f_out[to, ne + j] = column[j, req_sm[1, to * ROWS + j]]
        dst = f_in.at[pl.ds(s * (2 * ne), 2 * ne)]
        if d == 0:
            c = pltpu.make_async_copy(f_out.at[to], dst, f_loc)
        else:
            c = slab_copy(f_out.at[to], dst, f_send, f_recv, d)
        c.start()
        fetches.append(c)
    ask_copies = [
        event_copy(idx_req, asked_all.at[e], ask_send, ask_recv, d) for d in event_order
    ]
    for c in ask_copies:
        c.start()
    for c in id_copies + far + near:
        c.wait_send()

    owners = lax.shift_right_arithmetic(jnp.broadcast_to(ids_row, (LANES, LANES)), cfg_shift(blk))
    owners_t = jnp.transpose(owners)
    earlier = jnp.where((owners == owners_t) & (row_i < lane_i), 1, 0)
    rank = jnp.sum(earlier, axis=0, keepdims=True)
    owner_row = owners[0:1]
    at_e = owner_row // ns
    at_s = owner_row - at_e * ns
    live_n = live[0, 0]

    def in_order(lane):
        return lane % planes * tiles_y + lane // planes

    address = at_s * (2 * ne) + rank * ne + at_e
    alive = in_order(iota((1, LANES), 1)) < live_n
    address = jnp.where(alive, address, 2 * nb)
    none = LANES
    match = owners == row_i
    first = jnp.min(jnp.where(match, lane_i, none), axis=1, keepdims=True)
    second = jnp.min(jnp.where(match & (lane_i > first), lane_i, none), axis=1, keepdims=True)

    def tile_at(lane):
        tile = in_order(lane)
        return jnp.where((lane < none) & (tile < live_n), tile, n_tiles)

    tile_0 = tile_at(as_row(first))
    tile_1 = tile_at(as_row(second))
    idx_own[...] = jnp.where(
        sub == 0,
        jnp.broadcast_to(address, (ROWS, LANES)),
        jnp.where(
            sub == 1,
            jnp.broadcast_to(tile_0, (ROWS, LANES)),
            jnp.broadcast_to(tile_1, (ROWS, LANES)),
        ),
    )
    own_copy = pltpu.make_async_copy(idx_own, own_sm, idx_sem.at[0])
    own_copy.start()

    for c in load_weights:
        c.wait()
    high, low = split(stiff_y[...])
    w_y[...] = jnp.concatenate(
        [jnp.concatenate([high, high], axis=1), jnp.concatenate([low, low], axis=1)], axis=0
    )
    high, low = split(jnp.transpose(stiff_z[...]))
    half = jnp.concatenate([high, low], axis=1)
    w_z[...] = jnp.concatenate([half, half], axis=0)

    lax.fori_loop(reach, planes - reach, split_planes, 0, unroll=2)
    for side in range(2):

        @pl.when(s == (0 if side == 0 else ns - 1))
        def _():
            halo[:, 1 - side] = jnp.zeros((steps, reach) + u_a.shape[1:], BF16)

    half_rows = tiles_y * rows_b
    pick_b = jnp.where(iota((half_rows, rows_b), 0) % rows_b == iota((half_rows, rows_b), 1), 1.0, 0.0)
    pick_y = jnp.where(iota((rows_t, LANES), 1) % rows_t == iota((rows_t, LANES), 0), 1.0, 0.0)
    wide = dot(pick_b.astype(BF16), interp_y[...]).astype(BF16)
    wide = dot(wide, pick_y.astype(BF16))
    on_diag = iota((half_rows, LANES), 0) // rows_b == iota((half_rows, LANES), 1) // rows_t
    diag = jnp.where(on_diag, wide, 0.0)
    w_bwd[...] = diag.astype(BF16)
    w_fwd[...] = jnp.transpose(jnp.concatenate([diag, diag], axis=0)).astype(BF16)
    iz_t = jnp.transpose(interp_z[...].astype(F32)).astype(BF16)
    w_iz[...] = jnp.concatenate([iz_t, iz_t], axis=0)

    ny = LANES

    def stiff_pair(x):
        a, b = u_hl[x, 0], u_hl[x, 1]
        c, d = u_hl[x + 1, 0], u_hl[x + 1, 1]
        left = jnp.concatenate(
            [jnp.concatenate([a, b], axis=1), jnp.concatenate([c, d], axis=1)], axis=0
        )
        right = jnp.concatenate(
            [jnp.concatenate([a, c], axis=1), jnp.concatenate([b, d], axis=1)], axis=0
        )
        along_z = dot(left, w_z[...])
        along_z = along_z[:, :LANES] + along_z[:, LANES:]
        along_y = dot(w_y[...], right)
        along_y = along_y[:ny] + along_y[ny:]
        return along_z[:ny] + along_y[:, :LANES], along_z[ny:] + along_y[:, LANES:]

    def stencil(buf, x):
        total = coeffs[0, 0, x] * buf[x]
        for k in range(1, 2 * reach + 1):
            total = total + coeffs[k, 0, x] * buf[x + k]
        return total

    pairs = planes // 2
    edge = reach // 2

    def over_interior(body, unroll=12):
        def interior(i, carry):
            body(2 * i)
            return carry

        lax.fori_loop(edge, pairs - edge, interior, 0, unroll=unroll)

    def side_planes(side):
        return range(reach) if side == 0 else range(planes - reach, planes)

    def over_edge(body, side):
        start = 0 if side == 0 else pairs - edge

        def one(i, carry):
            body(2 * i)
            return carry

        lax.fori_loop(start, start + edge, one, 0, unroll=2)

    def own_part(buf, side):
        for x in side_planes(side)[::2]:
            for p, part in enumerate(stiff_pair(x)):
                total = part
                for k in range(2 * reach + 1):
                    if 0 <= x + p + k - reach < planes:
                        total = total + coeffs[k, 0, x + p] * buf[x + p + k]
                ku0[x + p] = total

    def whole_part(step, x):
        total = ku0[x]
        for k in range(2 * reach + 1):
            at = x + k - reach
            if at < 0:
                total = total + coeffs[k, 0, x] * halo[step, 1, at + reach].astype(F32)
            if at >= planes:
                total = total + coeffs[k, 0, x] * halo[step, 0, at - planes].astype(F32)
        return total

    def first_stiff(x):
        for p, part in enumerate(stiff_pair(x)):
            ku0[x + p] = part + stencil(u_a, x + p)

    load_coeffs.wait()
    over_interior(first_stiff)
    for side in range(2):
        own_part(u_a, side)
    for side in range(2):
        take_halo(0, side)
        for x in side_planes(side):
            ku0[x] = whole_part(0, x)
    f_in[2 * nb] = jnp.zeros(f_in.shape[1:], BF16)
    own_copy.wait()
    load_back.wait()
    load_prev.wait()
    for c in fetches[:-1]:
        c.wait_recv()
    for c in fetches[:-1]:
        c.wait_send()
    fetches[-1].wait()

    def speed_pair(x):
        blocks = jnp.concatenate(
            [f_in[own_sm[0, q * planes + x + p]] for p in range(2) for q in range(tiles_y)], axis=0
        )
        high, low = split(dot(blocks, interp_z[...]))
        right = jnp.concatenate(
            [
                jnp.concatenate([high[:half_rows], high[half_rows:]], axis=1),
                jnp.concatenate([low[:half_rows], low[half_rows:]], axis=1),
            ],
            axis=0,
        )
        perturb = dot(w_fwd[...], right)
        for p in range(2):
            speed[x + p] = speed[x + p] * jnp.exp(perturb[:, p * LANES : (p + 1) * LANES])

    def grad_pair(x):
        right = jnp.concatenate([u_hl[x, 1], u_hl[x + 1, 1]], axis=1)
        back = dot(w_bwd[...], right)
        parts = []
        for p in range(2):
            high, low = split(back[:, p * LANES : (p + 1) * LANES])
            parts.append(jnp.concatenate([high, low], axis=1))
        grads = dot(jnp.concatenate(parts, axis=0), w_iz[...])
        g_tiles[pl.ds(x * tiles_y, 2 * tiles_y)] = grads.astype(BF16).reshape(
            2 * tiles_y, rows_b, LANES
        )

    g_tiles[n_tiles] = jnp.zeros(g_tiles.shape[1:], BF16)

    def advance(x, force, step, now, prev):
        change = speed[x] * force
        drawn = adj[step, x] * change
        if step == steps - 1:
            ku0[x] = change
            u_hl[x, 1] = (kern[x] - drawn).astype(BF16)
            return
        if step == 0:
            kern[x] = -drawn
        else:
            kern[x] = kern[x] - drawn
        later = 2.0 * now[x + reach] - prev[x + reach] - change
        prev[x + reach] = later
        high, low = split(later)
        u_hl[x, 0] = high
        u_hl[x, 1] = low

    load_adj[0].wait()

    def first_step(x):
        speed_pair(x)
        for p in range(2):
            advance(x + p, ku0[x + p], 0, u_a, u_b)

    for side in range(2):
        over_edge(first_step, side)
        send_halo(1, side)
    over_interior(first_step)
    now, prev = u_b, u_a
    for step in range(1, steps):
        load_adj[step].wait()

        def body(x):
            parts = stiff_pair(x)
            for p in range(2):
                advance(x + p, parts[p] + stencil(now, x + p), step, now, prev)

        over_interior(body)
        for side in range(2):
            own_part(now, side)
        last = step == steps - 1
        if last:
            over_interior(grad_pair, 6)
        for i in range(2):
            side = (step + i) % 2
            take_halo(step, side)
            for x in side_planes(side):
                advance(x, whole_part(step, x), step, now, prev)
            if last:
                over_edge(grad_pair, side)
            else:
                send_halo(step + 1, side)
        now, prev = prev, now
    now, prev = prev, now

    events, slabs = event_order + [0], slab_order + [0]
    chunks = 2
    many_e, many_s = ne // chunks, ns // chunks

    def pack_event(d, h):
        to = event_at(d)
        part = pl.ds(h * many_s, many_s)
        for i in range(h * many_s, (h + 1) * many_s):
            g_a[to, i] = g_tiles[own_sm[1, to * ns + slab_at(slabs[i])]]
        src, dst = g_a.at[to, part], g_ra.at[e, part]
        if d == 0:
            return pltpu.make_async_copy(src, dst, g_loc.at[h])
        return event_copy(src, dst, ga1_send, ga1_recv, d, h * ne + d)

    def pack_slab(d, h):
        to = slab_at(d)
        part = pl.ds(h * many_e, many_e)
        for i in range(h * many_e, (h + 1) * many_e):
            g_b[to, i] = g_tiles[own_sm[2, event_at(events[i]) * ns + to]]
        src, dst = g_b.at[to, part], g_rb.at[s, part]
        if d == 0:
            return pltpu.make_async_copy(src, dst, g_loc.at[2 + h])
        return slab_copy(src, dst, gb1_send, gb1_recv, d, h * ns + d)

    a1, b1 = [], []
    for h in range(chunks):
        a1.append([])
        b1.append([])
        for i in range(max(ne, ns // 2)):
            for d in events[i : i + 1]:
                a1[h].append(pack_event(d, h))
                a1[h][-1].start()
            for d in slabs[2 * i : 2 * i + 2]:
                b1[h].append(pack_slab(d, h))
                b1[h][-1].start()
    a2, b2 = [], []
    for i, d in enumerate(slabs):
        if d == 0:
            a2.append(pltpu.make_async_copy(g_ra.at[:, i], g_in.at[0, :, s], g_loc.at[4]))
        else:
            a2.append(slab_copy(g_ra.at[:, i], g_in.at[0, :, s], ga2_send, ga2_recv, d))
    for i, d in enumerate(events):
        if d == 0:
            b2.append(pltpu.make_async_copy(g_rb.at[:, i], g_in.at[1, e], g_loc.at[5]))
        else:
            b2.append(event_copy(g_rb.at[:, i], g_in.at[1, e], gb2_send, gb2_recv, d))

    def arrive(copies):
        for c in copies[:-1]:
            c.wait_recv()
        copies[-1].wait()

    def last_wave(i, carry):
        prev[reach + i] = 2.0 * now[reach + i] - prev[reach + i] - ku0[i]
        return carry

    lax.fori_loop(0, planes, last_wave, 0)
    wave_copy = pltpu.make_async_copy(prev.at[pl.ds(reach, planes)], wave_out.at[0], out_sem)
    wave_copy.start()
    for h in range(chunks):
        arrive(a1[h])
        for c in a2[h * many_s : (h + 1) * many_s]:
            c.start()
        arrive(b1[h])
        for c in b2[h * many_e : (h + 1) * many_e]:
            c.start()

    for c in ask_copies:
        c.wait_recv()
    ranks = []
    for r in range(2):
        table = jnp.zeros((ROWS, LANES), I32)
        for i in range(ne):
            table = jnp.where(
                sub == i, jnp.broadcast_to(asked_all[i][r : r + 1], (ROWS, LANES)), table
            )
        ranks.append(table)
    width = ns * rows_b
    lane = iota((LANES, width), 1)
    pick = jnp.where(iota((LANES, width), 0) == lane // rows_b * ROWS + e, 1.0, 0.0)
    asked_both = jnp.concatenate(ranks, axis=0).astype(F32).astype(BF16)
    keys = dot(asked_both, pick.astype(BF16)).astype(I32) * rows_b
    keys = keys + iota((2 * ROWS, width), 1) % rows_b
    rows = iota((blk * rows_b, width), 0)
    for r in range(2):
        for i in range(ne):
            key = keys[r * ROWS + i : r * ROWS + i + 1]
            hot = jnp.where(jnp.broadcast_to(key, rows.shape) == rows, 1.0, 0.0)
            at = (r * ne + i) * width
            one_hot[:, at : at + width] = hot.astype(BF16)
    half_slots = nb * rows_b
    arrive(a2)
    total = dot(one_hot[:, :half_slots], g_in[0].reshape(half_slots, LANES))
    arrive(b2)
    total = total + dot(one_hot[:, half_slots:], g_in[1].reshape(half_slots, LANES))
    grad_out[...] = total.reshape(grad_out.shape)
    for h in range(chunks):
        for c in a1[h][:-1] + b1[h][:-1]:
            c.wait_send()
    for c in a2[:-1] + b2[:-1] + ask_copies:
        c.wait_send()
    wave_copy.wait()


def cfg_shift(blk):
    return blk.bit_length() - 1


def shards(
    wave_prev,
    wave_now,
    adjoint,
    background,
    coeffs_x,
    stiff_y,
    stiff_z,
    interp_y,
    interp_z,
    model,
    block_index,
    live_count,
):
    ne = lax.axis_size("event")
    ns = lax.axis_size("slab")
    nb = ne * ns
    blk, rows_b, _ = model.shape
    planes, ny, nz = wave_now.shape[1:]
    steps = adjoint.shape[1]
    reach = (coeffs_x.shape[2] - 1) // 2
    tiles_y = block_index.shape[2]
    n_tiles = planes * tiles_y
    rows_t = ny // tiles_y
    ids = jnp.swapaxes(block_index, 1, 2)
    coeffs = jnp.transpose(coeffs_x, (2, 0, 1))
    cfg = (ne, ns, planes, reach, steps, n_tiles, rows_t, blk, rows_b)
    arrays = (
        wave_prev,
        wave_now,
        adjoint,
        background,
        coeffs,
        live_count,
        stiff_y,
        stiff_z,
        interp_y,
        interp_z,
        model,
        ids,
    )
    arrays = [
        a if a is live_count else pltpu.with_memory_space_constraint(a, pltpu.HBM) for a in arrays
    ]
    dma = pltpu.SemaphoreType.DMA
    vmem = pltpu.VMEM
    slot = (rows_b, nz)

    def buffers():
        return [
            vmem((ne, ns) + slot, BF16),
            vmem((ns, ne) + slot, BF16),
            vmem((ne, ns) + slot, BF16),
            vmem((ns, ne) + slot, BF16),
        ]

    def sems():
        return [dma((n,)) for n in (2 * ne, 2 * ne, ns, ns, 2 * ns, 2 * ns, ne, ne)] + [dma((6,))]

    grads = buffers()
    whole = pl.BlockSpec(memory_space=pltpu.VMEM)
    smem = pl.BlockSpec(memory_space=pltpu.SMEM)
    hbm = pl.BlockSpec(memory_space=pltpu.HBM)
    free = pl.BlockSpec(memory_space=pl.ANY)
    wave, grad = pl.pallas_call(
        functools.partial(window_kernel, cfg),
        out_shape=(
            jax.ShapeDtypeStruct(wave_now.shape, F32),
            jax.ShapeDtypeStruct(model.shape, F32),
        ),
        in_specs=[hbm] * 5 + [smem] + [hbm] * 6,
        out_specs=(free, whole),
        scratch_shapes=[
            vmem((planes + 2 * reach, ny, nz), F32),
            vmem((planes + 2 * reach, ny, nz), F32),
            vmem((planes, 2, ny, nz), BF16),
            vmem((planes, ny, nz), F32),
            vmem((planes, ny, nz), F32),
            vmem((steps, planes, ny, nz), F32),
            vmem((planes, ny, nz), F32),
            vmem((steps, 2, reach, ny, nz), BF16),
            vmem((2 * ny, 2 * ny), BF16),
            vmem((2 * nz, 2 * nz), BF16),
            vmem((ny, 2 * tiles_y * rows_b), BF16),
            vmem((tiles_y * rows_b, ny), BF16),
            vmem((2 * nz, nz), BF16),
            pltpu.SMEM(coeffs.shape, F32),
            vmem(stiff_y.shape, F32),
            vmem(stiff_z.shape, F32),
            vmem(interp_y.shape, BF16),
            vmem(interp_z.shape, BF16),
            vmem(ids.shape, I32),
            vmem((ROWS, LANES), I32),
            vmem((LANES // ROWS, ROWS, LANES), I32),
            vmem((ROWS, LANES), I32),
            vmem((ROWS, LANES), I32),
            vmem((ne, ROWS, LANES), I32),
            pltpu.SMEM((ROWS, LANES), I32),
            pltpu.SMEM((ROWS, LANES), I32),
            vmem((ne,) + model.shape, BF16),
            vmem((ns, 2 * ne) + slot, BF16),
            vmem((2 * nb + 1,) + slot, BF16),
            vmem((n_tiles + 1,) + slot, BF16),
            *grads,
            vmem((2, ne, ns) + slot, BF16),
            vmem((blk * rows_b, 2 * nb * rows_b), BF16),
            dma((3 + steps,)),
            dma((6,)),
            dma((3,)),
            dma((ns,)),
            dma((ns,)),
            dma((ne,)),
            dma((ne,)),
            dma((ne // 2,)),
            dma((ne // 2,)),
            dma((ne,)),
            dma((ne,)),
            dma((ns,)),
            dma((ns,)),
            dma((steps, 2)),
            dma((steps, 2)),
            dma,
            *sems(),
            dma,
        ],
        compiler_params=pltpu.CompilerParams(
            collective_id=0, has_side_effects=True, vmem_limit_bytes=40 * 1024 * 1024
        ),
        name="window",
    )(*arrays)
    return wave, grad


def solution(mesh):
    return jax.shard_map(
        shards,
        mesh=mesh,
        in_specs=(
            P("event", "slab", None, None),
            P("event", "slab", None, None),
            P("event", None, "slab", None, None),
            P("event", "slab", None, None),
            P("event", "slab", None),
            P(),
            P(),
            P(),
            P(),
            P(("event", "slab"), None, None),
            P("event", "slab", None),
            P("event", "slab"),
        ),
        out_specs=(P("event", "slab", None, None), P(("event", "slab"), None, None)),
        check_vma=False,
    )
```
